32 devices in a mesh: hour: 16 (over z, y, x), region: 2 (over core).
Axes of the slice: x: 2, y: 2, z: 4, core: 2. Of those that a mesh axis runs over, the one named last changes fastest.
Arguments:
- demand: float32 [2240, 1024], P('hour', 'region'), may hold values from 0.2 to 2
- avail_factor: bfloat16 [2240, 8, 1024], P('hour', None, 'region'), may hold values from 0 to 1
- tech_mask: int32 [8, 1024], P(None, 'region'), may hold values 0 or 1
- var_cost: float32 [8, 1024], P(None, 'region'), may hold values from 0.1 to 2
- inv_cost: float32 [8, 1024], P(None, 'region'), may hold values from 0.2 to 1
- ramp_rate: float32 [8, 1024], P(None, 'region'), may hold values from 0.1 to 1
- network: float32 [1024, 1024], P('region'), as said below
- pattern: int32 [8, 8], replicated, may hold values from 0 to 1, as said below
- live_hours: int32 [1], replicated, may hold values from 1961 to 2100
- generation: float32 [2240, 8, 1024], P('hour', None, 'region'), may hold values from 0 to 1
- angles: float32 [2240, 1024], P('hour', 'region'), may hold values from -3 to 3
- levels: float32 [2240, 1024], P('hour', 'region'), may hold values from 0 to 2
- net_power: float32 [2240, 1024], P('hour', 'region'), may hold values from -3 to 3
- capacity: float32 [8, 1024], P(None, 'region'), may hold values from 0.5 to 2
- balance_dual: float32 [2240, 1024], P('hour', 'region'), may hold values from -3 to 3
- storage_dual: float32 [2240, 1024], P('hour', 'region'), may hold values from -3 to 3
- limit_dual: float32 [2240, 8, 1024], P('hour', None, 'region'), may hold values from 0 to 1.5
- ramp_dual: float32 [2240, 8, 1024], P('hour', None, 'region'), may hold values from 0 to 0.5
Outputs:
- final_generation: float32 [2240, 8, 1024], P('hour', None, 'region')
- final_angles: float32 [2240, 1024], P('hour', 'region')
- final_levels: float32 [2240, 1024], P('hour', 'region')
- final_power: float32 [2240, 1024], P('hour', 'region')
- final_capacity: float32 [8, 1024], P(None, 'region')
- final_balance: float32 [2240, 1024], P('hour', 'region')
- final_storage: float32 [2240, 1024], P('hour', 'region')
- final_limit: float32 [2240, 8, 1024], P('hour', None, 'region')
- final_ramp: float32 [2240, 8, 1024], P('hour', None, 'region')
The draws below stay inside these ranges and needn't reach their ends.
Inputs may be any that keep to these rules, and one draw needn't show every extreme that they name: pattern is symmetric with ones on its diagonal. network is symmetric.
All inputs are finite; a program needn't handle non-finite values. No bound on the sum of `tech_mask` on one device may be relied on, other than what follows from the above.
Results may differ from the reference program's by a relative error of at most 0.0003.
Values sent between devices are 32-bit elements; how exact they have to be, the bound alone decides.
No kernel may reach another device: no remote copies, remote signals or barrier semaphores. Data moves between devices by JAX's collectives and lax.ppermute only.
A program may use at most 64 MiB of HBM per device.

```python
import math
import jax
import jax.numpy as jnp
from jax import lax

HOUR_DEV = 140
BUS = 1024
TECH = 8
BLOCK = 128
ITERS = 2
HOURS = 2240
NBB = 8


def draw_network(key, part):
    values = jax.random.normal(key, (BUS, BUS), jnp.float32)
    return (values + values.T) * (0.5 * BUS ** (-0.5)) + jnp.eye(BUS, dtype=jnp.float32)


def draw_pattern(key, part):
    coupled = jax.random.randint(key, (NBB, NBB), 0, 2).astype(jnp.int32)
    symmetric = jnp.maximum(coupled, coupled.T)
    indices = jnp.arange(NBB, dtype=jnp.int32)
    diagonal = (indices[:, None] == indices[None, :]).astype(jnp.int32)
    return jnp.maximum(symmetric, diagonal)


def draw_limit_dual(key, part):
    values = jax.random.uniform(key, (HOURS, TECH, BUS), jnp.float32, 0.0, 0.5)
    rising = 1.0 + 2.0 * jnp.arange(HOURS, dtype=jnp.float32) / float(HOURS - 1)
    return values * rising[:, None, None]


def plant(result, key, low, high):
    extent = result.shape
    index_at = [jax.random.randint(jax.random.fold_in(key, axis), (), 0, extent[axis]) for axis in range(len(extent))]
    result = result.at[tuple(index_at)].set(low)
    longest = extent.index(max(extent))
    index_at[longest] = (index_at[longest] + 1) % extent[longest]
    return result.at[tuple(index_at)].set(high)


def shard_levels(rng, extent, cuts, least, high):
    def one(axis_at, blocks):
        heights = jax.random.uniform(jax.random.fold_in(jax.random.fold_in(rng, 6), axis_at), (blocks,), jnp.float32, least / len(cuts), high / len(cuts))
        return jnp.repeat(jnp.exp(heights), extent[axis_at] // blocks).reshape((-1,) + (1,) * (len(extent) - axis_at - 1))

    level = one(*cuts[0])
    for cut in cuts[1:]:
        level = level * one(*cut)
    return level


def centred(stream_key, extent, deviation, most, cuts=(), held_as=jnp.bfloat16):
    gain = shard_levels(stream_key, extent, cuts, -0.22, 0.18) if cuts else 1.0
    entries = jax.random.normal(stream_key, extent, jnp.float32) * deviation * gain
    return jnp.minimum(jnp.maximum(entries, -most), most).astype(held_as)


def setup_inputs(seed: int = 0) -> dict:
    seeds = jax.random.split(jax.random.key(seed), 19)
    return {
        "demand": jnp.clip(jnp.exp(math.log(2.0) - 2.3025851 * jax.random.uniform(seeds[0], (HOURS, BUS), jnp.float32) ** shard_levels(seeds[0], (HOURS, BUS), ((0, 16), (1, 2)), -0.2, 0.2)), 0.2, 2.0),
        "avail_factor": jnp.clip(1.0 * jax.random.uniform(seeds[1], (HOURS, TECH, BUS), jnp.float32) ** shard_levels(seeds[1], (HOURS, TECH, BUS), ((0, 16), (2, 2)), -0.2, 0.2), 0.0, 1.0).astype(jnp.bfloat16),
        "tech_mask": plant((jax.random.randint(seeds[2], (TECH, BUS), 0, 4) < 3).astype(jnp.int32), jax.random.fold_in(seeds[2], 1), 0, 1),
        "var_cost": jnp.clip(jnp.exp(math.log(2.0) - 2.9957323 * jax.random.uniform(seeds[3], (TECH, BUS), jnp.float32) ** shard_levels(seeds[3], (TECH, BUS), ((1, 2),), -0.2, 0.2)), 0.1, 2.0),
        "inv_cost": jnp.clip(jnp.exp(math.log(1.0) - 1.609438 * jax.random.uniform(seeds[4], (TECH, BUS), jnp.float32) ** shard_levels(seeds[4], (TECH, BUS), ((1, 2),), -0.2, 0.2)), 0.2, 1.0),
        "ramp_rate": jnp.clip(jnp.exp(math.log(1.0) - 2.3025851 * jax.random.uniform(seeds[5], (TECH, BUS), jnp.float32) ** shard_levels(seeds[5], (TECH, BUS), ((1, 2),), -0.2, 0.2)), 0.1, 1.0),
        "network": draw_network(jax.random.fold_in(seeds[18], 71), 0),
        "pattern": draw_pattern(jax.random.fold_in(seeds[18], 71), 0),
        "live_hours": jax.random.randint(seeds[8], (1,), HOURS - 2 * HOUR_DEV + 1, HOURS - HOUR_DEV + 1).astype(jnp.int32),
        "generation": jnp.clip(1.0 * jax.random.uniform(seeds[9], (HOURS, TECH, BUS), jnp.float32) ** shard_levels(seeds[9], (HOURS, TECH, BUS), ((0, 16), (2, 2)), -0.2, 0.2), 0.0, 1.0),
        "angles": centred(seeds[10], (HOURS, BUS), 0.5, 3.0, ((0, 16), (1, 2)), jnp.float32),
        "levels": jnp.clip(2.0 * jax.random.uniform(seeds[11], (HOURS, BUS), jnp.float32) ** shard_levels(seeds[11], (HOURS, BUS), ((0, 16), (1, 2)), -0.2, 0.2), 0.0, 2.0),
        "net_power": centred(seeds[12], (HOURS, BUS), 0.5, 3.0, ((0, 16), (1, 2)), jnp.float32),
        "capacity": jnp.clip(0.5 + 1.5 * jax.random.uniform(seeds[13], (TECH, BUS), jnp.float32) ** shard_levels(seeds[13], (TECH, BUS), ((1, 2),), -0.2, 0.2), 0.5, 2.0),
        "balance_dual": centred(seeds[14], (HOURS, BUS), 0.5, 3.0, ((0, 16), (1, 2)), jnp.float32),
        "storage_dual": centred(seeds[15], (HOURS, BUS), 0.5, 3.0, ((0, 16), (1, 2)), jnp.float32),
        "limit_dual": draw_limit_dual(jax.random.fold_in(seeds[18], 71), 0),
        "ramp_dual": jnp.clip(0.5 * jax.random.uniform(seeds[17], (HOURS, TECH, BUS), jnp.float32) ** shard_levels(seeds[17], (HOURS, TECH, BUS), ((0, 16), (2, 2)), -0.2, 0.2), 0.0, 0.5),
    }


primal_step = 0.2
capacity_step = 4.0
dual_scale = 0.06

def reference(demand, avail_factor, tech_mask, var_cost, inv_cost, ramp_rate, network, pattern, live_hours, generation, angles, levels, net_power, capacity, balance_dual, storage_dual, limit_dual, ramp_dual):
    hour_count = demand.shape[0]
    live_rows = (jnp.arange(hour_count, dtype=jnp.int32) < live_hours[0]).astype(jnp.float32)
    available = avail_factor.astype(jnp.float32) * tech_mask.astype(jnp.float32)[None] * live_rows[:, None, None]
    live_load = demand * live_rows[:, None]
    block_mask = jnp.repeat(jnp.repeat(pattern.astype(jnp.float32), BLOCK, 0), BLOCK, 1)
    matrix = network * block_mask

    def apply_network(source):
        return jnp.dot(source, matrix.T, precision=lax.Precision.HIGHEST, preferred_element_type=jnp.float32)
    entry_count = float(HOURS * (TECH + 3) * BUS)
    for iteration in range(ITERS):
        prev_ramp = jnp.roll(ramp_dual, 1, axis=0)
        prev_store = jnp.roll(storage_dual, 1, axis=0)
        gen_new = jnp.maximum(0.0, generation - primal_step * (var_cost[None] + balance_dual[:, None, :] + limit_dual + prev_ramp - ramp_dual))
        ang_new = angles + primal_step * apply_network(balance_dual)
        pow_new = net_power - primal_step * (balance_dual + storage_dual)
        lev_new = jnp.maximum(0.0, levels - primal_step * (prev_store - storage_dual))
        invest = lax.optimization_barrier(jnp.sum(available * limit_dual + ramp_rate[None] * ramp_dual, axis=0))
        cap_new = jnp.maximum(0.0, capacity - capacity_step * (inv_cost - invest / float(HOURS)))
        squares = jnp.sum((gen_new - generation) ** 2) + jnp.sum((ang_new - angles) ** 2) + jnp.sum((pow_new - net_power) ** 2) + jnp.sum((lev_new - levels) ** 2)
        step_size = jnp.sqrt(squares / entry_count + 1e-06)
        dual_step = dual_scale / step_size
        gen_bar = 2.0 * gen_new - generation
        ang_bar = 2.0 * ang_new - angles
        pow_bar = 2.0 * pow_new - net_power
        lev_bar = 2.0 * lev_new - levels
        cap_bar = 2.0 * cap_new - capacity
        balance_dual = balance_dual + dual_step * (lax.optimization_barrier(jnp.sum(gen_bar, axis=1)) + pow_bar - apply_network(ang_bar) - live_load)
        storage_dual = storage_dual + dual_step * (jnp.roll(lev_bar, -1, axis=0) - lev_bar + pow_bar)
        limit_dual = jnp.maximum(0.0, limit_dual + dual_step * (gen_bar - available * cap_bar[None]))
        ramp_dual = jnp.maximum(0.0, ramp_dual + dual_step * (jnp.roll(gen_bar, -1, axis=0) - gen_bar - ramp_rate[None] * cap_bar[None]))
        generation, angles, net_power, levels, capacity = (gen_new, ang_new, pow_new, lev_new, cap_new)
    return (generation, angles, levels, net_power, capacity, balance_dual, storage_dual, limit_dual, ramp_dual)
```

```python
import jax
import jax.numpy as jnp
from jax import lax
from jax.sharding import PartitionSpec as P

BUS = 1024
TECH = 8
BLOCK = 128
ITERS = 2


primal_step = 0.2
capacity_step = 4.0
dual_scale = 0.06


def shifted(block, axis, distance):
    devices = range(lax.axis_size(axis))
    route = [((i - distance) % len(devices), i) for i in devices]
    return lax.ppermute(block, axis, route)


def summed(block, axis):
    size = lax.axis_size(axis)
    distance = 1
    while distance < size:
        route = [(i, i ^ distance) for i in range(size)]
        block = block + lax.ppermute(block, axis, route)
        distance *= 2
    return block


def per_device(
    demand,
    avail_factor,
    tech_mask,
    var_cost,
    inv_cost,
    ramp_rate,
    network,
    pattern,
    live_hours,
    generation,
    angles,
    levels,
    net_power,
    capacity,
    balance_dual,
    storage_dual,
    limit_dual,
    ramp_dual,
):
    hour_rows = demand.shape[0]
    local_bus = demand.shape[1]
    total_hours = hour_rows * lax.axis_size("hour")
    first_hour = lax.axis_index("hour") * hour_rows
    live_rows = (first_hour + jnp.arange(hour_rows, dtype=jnp.int32) < live_hours[0]).astype(
        jnp.float32
    )
    available = (
        avail_factor.astype(jnp.float32)
        * tech_mask.astype(jnp.float32)[None]
        * live_rows[:, None, None]
    )
    live_load = demand * live_rows[:, None]
    blocks_here = local_bus // BLOCK
    pattern_rows = lax.dynamic_slice_in_dim(
        pattern, lax.axis_index("region") * blocks_here, blocks_here, 0
    )
    block_mask = jnp.repeat(jnp.repeat(pattern_rows.astype(jnp.float32), BLOCK, 0), BLOCK, 1)
    matrix = network * block_mask
    entry_count = float(total_hours * (TECH + 3) * BUS)

    def fold_part(segment):
        return lax.dot_general(
            segment,
            matrix,
            (((1,), (1,)), ((), ())),
            precision=lax.Precision.HIGHEST,
            preferred_element_type=jnp.float32,
        )

    for iteration in range(ITERS):
        behind = shifted((ramp_dual[-1:], storage_dual[-1:]), "hour", 1)
        prev_ramp = jnp.concatenate([behind[0], ramp_dual[:-1]], axis=0)
        prev_store = jnp.concatenate([behind[1], storage_dual[:-1]], axis=0)
        gen_new = jnp.maximum(
            0.0,
            generation
            - primal_step
            * (var_cost[None] + balance_dual[:, None, :] + limit_dual + prev_ramp - ramp_dual),
        )
        ang_new = angles + primal_step * fold_part(
            lax.all_gather(balance_dual, "region", axis=1, tiled=True)
        )
        pow_new = net_power - primal_step * (balance_dual + storage_dual)
        lev_new = jnp.maximum(0.0, levels - primal_step * (prev_store - storage_dual))
        square_part = (
            jnp.sum((gen_new - generation) ** 2)
            + jnp.sum((ang_new - angles) ** 2)
            + jnp.sum((pow_new - net_power) ** 2)
            + jnp.sum((lev_new - levels) ** 2)
        )
        invest_part = jnp.sum(available * limit_dual + ramp_rate[None] * ramp_dual, axis=0)
        square_part = summed(jnp.full((8, invest_part.shape[1]), square_part), "region")
        totals = summed(jnp.concatenate([invest_part, square_part], axis=0), "hour")
        invest = totals[:TECH]
        squares = totals[TECH, 0]
        cap_new = jnp.maximum(
            0.0, capacity - capacity_step * (inv_cost - invest / float(total_hours))
        )
        step_size = jnp.sqrt(squares / entry_count + 1e-06)
        dual_step = dual_scale / step_size
        gen_bar = 2.0 * gen_new - generation
        ang_bar = 2.0 * ang_new - angles
        pow_bar = 2.0 * pow_new - net_power
        lev_bar = 2.0 * lev_new - levels
        cap_bar = 2.0 * cap_new - capacity
        forward = shifted((gen_bar[:1], lev_bar[:1]), "hour", -1)
        next_gen = jnp.concatenate([gen_bar[1:], forward[0]], axis=0)
        next_level = jnp.concatenate([lev_bar[1:], forward[1]], axis=0)
        balance_dual = balance_dual + dual_step * (
            jnp.sum(gen_bar, axis=1)
            + pow_bar
            - fold_part(lax.all_gather(ang_bar, "region", axis=1, tiled=True))
            - live_load
        )
        storage_dual = storage_dual + dual_step * (next_level - lev_bar + pow_bar)
        limit_dual = jnp.maximum(
            0.0, limit_dual + dual_step * (gen_bar - available * cap_bar[None])
        )
        ramp_dual = jnp.maximum(
            0.0, ramp_dual + dual_step * (next_gen - gen_bar - ramp_rate[None] * cap_bar[None])
        )
        generation, angles, net_power, levels, capacity = (
            gen_new,
            ang_new,
            pow_new,
            lev_new,
            cap_new,
        )
    return (
        generation,
        angles,
        levels,
        net_power,
        capacity,
        balance_dual,
        storage_dual,
        limit_dual,
        ramp_dual,
    )


def solution(mesh):
    return jax.shard_map(
        per_device,
        mesh=mesh,
        in_specs=(
            P("hour", "region"),
            P("hour", None, "region"),
            P(None, "region"),
            P(None, "region"),
            P(None, "region"),
            P(None, "region"),
            P("region", None),
            P(),
            P(),
            P("hour", None, "region"),
            P("hour", "region"),
            P("hour", "region"),
            P("hour", "region"),
            P(None, "region"),
            P("hour", "region"),
            P("hour", "region"),
            P("hour", None, "region"),
            P("hour", None, "region"),
        ),
        out_specs=(
            P("hour", None, "region"),
            P("hour", "region"),
            P("hour", "region"),
            P("hour", "region"),
            P(None, "region"),
            P("hour", "region"),
            P("hour", "region"),
            P("hour", None, "region"),
            P("hour", None, "region"),
        ),
        check_vma=False,
    )
```

```python
import functools

import jax
import jax.numpy as jnp
from jax import lax
from jax.experimental import pallas as pl
from jax.experimental.pallas import tpu as pltpu
from jax.sharding import PartitionSpec as P

BUS = 1024
TECH = 8
BLOCK = 128
ITERS = 2

primal_step = 0.2
capacity_step = 4.0
dual_scale = 0.06

F32 = jnp.float32
VMEM = pl.BlockSpec(memory_space=pltpu.VMEM)
SMEM = pl.BlockSpec(memory_space=pltpu.SMEM)
HBM = pl.BlockSpec(memory_space=pltpu.HBM)


def shifted(block, axis, distance):
    devices = range(lax.axis_size(axis))
    route = [((i - distance) % len(devices), i) for i in devices]
    return lax.ppermute(block, axis, route)


def partner(block, axis, distance):
    return lax.ppermute(block, axis, [(i, i ^ distance) for i in range(lax.axis_size(axis))])


def distances(axis):
    size = lax.axis_size(axis)
    return [1 << i for i in range(size.bit_length() - 1)]


def summed(block, axis):
    for distance in distances(axis):
        block = block + partner(block, axis, distance)
    return block


def after(block, earlier):
    return lax.optimization_barrier((block, earlier))[0]


def divisor(extent, most):
    return max(d for d in range(1, most + 1) if extent % d == 0)


def split(value):
    high = value.astype(jnp.bfloat16)
    return high, (value - high.astype(F32)).astype(jnp.bfloat16)


def network_product(sources, high_ref, low_ref):
    total, at = None, 0
    for source in sources:
        columns = slice(at, at + source.shape[1])
        at += source.shape[1]
        high, low = split(source[...])
        for left, right in ((high, high_ref), (low, high_ref), (high, low_ref)):
            term = lax.dot_general(
                left, right[:, columns], (((1,), (1,)), ((), ())), preferred_element_type=F32
            )
            total = term if total is None else total + term
    return total


def call(body, operands, specs, outs, out_specs=None, scratch=(), flops=1 << 22, moved=1 << 23, room=8, name=None):
    operands = [
        pltpu.with_memory_space_constraint(operand, pltpu.HBM) if spec is HBM else operand
        for operand, spec in zip(operands, specs)
    ]
    return pl.pallas_call(
        body,
        out_shape=[jax.ShapeDtypeStruct(shape, dtype) for shape, dtype in outs],
        in_specs=specs,
        out_specs=out_specs or [VMEM] * len(outs),
        scratch_shapes=list(scratch),
        compiler_params=pltpu.CompilerParams(vmem_limit_bytes=room << 20),
        cost_estimate=pl.CostEstimate(flops=flops, bytes_accessed=moved, transcendentals=0),
        name=name,
    )(*operands)


def load_body(
    swap, gen_h, lim_h, ramp_h, av_h, net_h, mask_h, vc_h, rr_h, bal_h, demand_h, pat_h, live_s,
    bar_ref, new_ref, lim_ref, ramp_ref, avail_ref, high_ref, low_ref, invest_ref, square_ref, load_ref,
    av_v, net_v, mask_v, vc_v, rr_v, bal_v, demand_v, pat_s, sems, net_sem, small_sem,
):
    rows, _, buses = gen_h.shape
    chunk = divisor(rows, 28)
    unroll = divisor(chunk, 7)
    chunks = rows // chunk
    region = lax.axis_index("region")
    pieces = 2 if swap else 1
    width = BUS // pieces

    def network_copy(piece):
        at = pl.multiple_of(lax.rem(region + piece, pieces) * width, BLOCK) if swap else 0
        return pltpu.make_async_copy(
            net_h.at[:, pl.ds(at, width)], net_v.at[:, pl.ds(piece * width, width)], net_sem.at[piece]
        )

    def copies(i):
        rows_here = pl.ds(i * chunk, chunk)
        return [
            pltpu.make_async_copy(source.at[rows_here], target.at[rows_here], sems.at[i, k])
            for k, (source, target) in enumerate(
                ((gen_h, bar_ref), (lim_h, lim_ref), (ramp_h, ramp_ref), (av_h, av_v))
            )
        ]

    small = [
        pltpu.make_async_copy(source, target, small_sem.at[k])
        for k, (source, target) in enumerate(
            ((pat_h, pat_s), (mask_h, mask_v), (vc_h, vc_v), (rr_h, rr_v), (bal_h, bal_v),
             (demand_h, demand_v))
        )
    ]
    for copy in small[:-1]:
        copy.start()
    for piece in range(pieces):
        network_copy(piece).start()
    for i in range(chunks):
        for copy in copies(i):
            copy.start()
    small[-1].start()

    for copy in small[:-1]:
        copy.wait()
    blocks = buses // BLOCK
    shift = region * blocks if swap else 0
    for piece in range(pieces):
        network_copy(piece).wait()
        for i in range(blocks):
            for j in range(piece * width // BLOCK, (piece + 1) * width // BLOCK):
                at = (slice(i * BLOCK, (i + 1) * BLOCK), slice(j * BLOCK, (j + 1) * BLOCK))
                coupled = pat_s[region * blocks + i, lax.rem(j + shift, BUS // BLOCK)].astype(F32)
                high, low = split(net_v[at] * coupled)
                high_ref[at] = high
                low_ref[at] = low

    mask = mask_v[...].astype(F32)
    cost = vc_v[...]
    live = live_s[0] - lax.axis_index("hour") * rows

    def step(t, carry, first=False):
        before, limit_sum, ramp_sum, squares = carry
        gen, lim, ramp = bar_ref[t], lim_ref[t], ramp_ref[t]
        alive = jnp.where(t < live, 1.0, 0.0).astype(F32)
        avail = av_v[t].astype(F32) * mask * alive
        avail_ref[t] = avail
        limit_sum += avail * lim
        ramp_sum += ramp
        if not first:
            dual = jnp.broadcast_to(bal_v[pl.ds(t, 1), :], (TECH, buses))
            new = jnp.maximum(0.0, gen - primal_step * (cost + dual + lim + before - ramp))
            squares += (new - gen) ** 2
            new_ref[t] = new
            bar_ref[t] = 2.0 * new - gen
        return ramp, limit_sum, ramp_sum, squares

    carry = (jnp.zeros((TECH, buses), F32),) * 4
    for i in range(chunks):
        for copy in copies(i):
            copy.wait()
        start = i * chunk
        if i == 0:
            for t in range(unroll):
                carry = step(t, carry, t == 0)
            start = unroll

        def several(j, carry, start=start):
            for k in range(unroll):
                carry = step(start + j * unroll + k, carry)
            return carry

        carry = lax.fori_loop(0, ((i + 1) * chunk - start) // unroll, several, carry)
    _, limit_sum, ramp_sum, squares = carry
    invest_ref[...] = limit_sum + rr_v[...] * ramp_sum
    square_ref[...] = squares
    small[-1].wait()
    row = lax.broadcasted_iota(jnp.int32, (rows, buses), 0)
    load_ref[...] = jnp.where(row < live, demand_v[...], 0.0)


def fold_rows(square):
    rows = square.shape[0]
    full = rows // TECH * TECH
    total = jnp.sum(square[:full].reshape(full // TECH, TECH, square.shape[1]), axis=0)
    return total, square[full:]


def put_totals(out_ref, invest, squares, rows_of_one, cubes):
    buses = invest.shape[1]
    out_ref[:, :buses] = invest
    lone = [jnp.sum(squares, axis=0, keepdims=True), *rows_of_one]
    for i, row in enumerate(lone):
        out_ref[i : i + 1, buses : 2 * buses] = row
    out_ref[len(lone) :, buses : 2 * buses] = jnp.zeros((TECH - len(lone), buses), F32)
    for i, cube in enumerate(cubes):
        out_ref[:, (i + 2) * buses : (i + 3) * buses] = cube


def get_totals(entries, buses, here_ref, squares_ref, other_ref):
    squares = jnp.sum(squares_ref[0:1, buses : 2 * buses] + other_ref[0:1, buses : 2 * buses])
    return here_ref[:, :buses], dual_scale * lax.rsqrt(jnp.full((1, 1), squares / entries + 1e-06, F32))


def neighbour(passed, ahead, index):
    device = lax.axis_index("hour")
    block = passed[0][index]
    for k in range(1, len(passed)):
        low = lax.rem(device, 1 << k)
        differs = low == (1 << k) - 1 if ahead else low == 0
        block = jnp.where(differs, passed[k][index], block)
    return block


def add_squares(total, *terms):
    for term in terms:
        full, rest = fold_rows(term * term)
        total = total + full
        if rest.shape[0]:
            rest = jnp.sum(rest, axis=0, keepdims=True)
            row = lax.broadcasted_iota(jnp.int32, total.shape, 0)
            total = total + jnp.where(row == 0, rest, 0.0)
    return total


def first_body(
    pieces, bar_ref, lim_ref, ramp_ref, halo_ref, vc_ref, invest_ref, square_ref, bal_ref, *refs,
):
    others, refs = refs[: pieces], refs[pieces:]
    (
        ang_ref, pow_ref, lev_ref, sto_ref, high_ref, low_ref,
        row_ref, flow_ref, angbar_ref, pownew_ref, powbar_ref, levnew_ref, levbar_ref,
        total_ref, shift_ref,
    ) = refs
    rows, _, buses = bar_ref.shape
    gen = bar_ref[0]
    dual = jnp.broadcast_to(bal_ref[0:1, :], (TECH, buses))
    new = jnp.maximum(
        0.0, gen - primal_step * (vc_ref[...] + dual + lim_ref[0] + halo_ref[:TECH] - ramp_ref[0])
    )
    row_ref[...] = new
    bal, sto = bal_ref[...], sto_ref[...]
    flow = network_product(others, high_ref, low_ref)
    flow_ref[...] = flow
    ang_step = primal_step * flow
    angbar_ref[...] = ang_ref[...] + 2.0 * ang_step
    pow_old = pow_ref[...]
    pow_new = pow_old - primal_step * (bal + sto)
    pownew_ref[...] = pow_new
    powbar_ref[...] = 2.0 * pow_new - pow_old
    shift_ref[8 : 8 + rows] = sto
    shift_ref[7:8] = halo_ref[TECH : TECH + 1]
    lev_old = lev_ref[...]
    lev_new = jnp.maximum(0.0, lev_old - primal_step * (shift_ref[7 : 7 + rows] - sto))
    levnew_ref[...] = lev_new
    levbar_ref[...] = 2.0 * lev_new - lev_old
    squares = add_squares(
        square_ref[...], new - gen, ang_step, pow_new - pow_old, lev_new - lev_old
    )
    put_totals(
        total_ref, invest_ref[...], squares,
        (levbar_ref[0:1], levbar_ref[rows - 1 : rows], powbar_ref[rows - 1 : rows]),
        (2.0 * new - gen, bar_ref[rows - 1]),
    )


def residual_one_body(
    pieces, bar_ref, total_ref, powbar_ref, load_ref, high_ref, low_ref, *refs,
):
    sources, (out_ref, sum_ref) = refs[:pieces], refs[pieces:]
    rows, _, buses = bar_ref.shape
    unroll = divisor(rows, 7)
    flow = network_product(sources, high_ref, low_ref)

    def several(j, _):
        for k in range(unroll):
            t = j * unroll + k
            sum_ref[pl.ds(t, 1), :] = jnp.sum(bar_ref[t], axis=0, keepdims=True)
        return 0

    lax.fori_loop(0, rows // unroll, several, 0)
    sum_ref[0:1] = jnp.sum(total_ref[:, 2 * buses : 3 * buses], axis=0, keepdims=True)
    out_ref[...] = sum_ref[...] + powbar_ref[...] - flow - load_ref[...]


def product_body(pieces, high_ref, low_ref, *refs):
    refs[pieces][...] = network_product(refs[:pieces], high_ref, low_ref)


def capacity_of(hours, cap_ref, inv_ref, invest):
    return jnp.maximum(0.0, cap_ref[...] - capacity_step * (inv_ref[...] - invest / float(hours)))


def middle_body(
    hours, entries, steps, here_ref, squares_ref, other_ref, mine_ref, *refs,
):
    passed, refs = refs[:steps], refs[steps:]
    (
        cap_ref, inv_ref, rr_ref, vc_ref,
        bar_ref, new_ref, row_ref, lim_ref, ramp_ref, avail_ref, halo_ref,
        bal_ref, res_ref, resflow_ref, flow_ref, ang_ref, pownew_ref, powbar_ref, levnew_ref, levbar_ref, sto_ref,
        capout_ref, gen2_ref, lim2_ref, ramp2_ref, bal2_ref, sto2_ref, ang2_ref, angbar2_ref, pow2_ref,
        powbar2_ref, lev2_ref, levbar2_ref, out_ref, shift_ref,
    ) = refs
    rows, _, buses = bar_ref.shape
    invest, step_size = get_totals(entries, buses, here_ref, squares_ref, other_ref)

    def lone(ahead, row):
        return neighbour(passed, ahead, (slice(row, row + 1), slice(buses, 2 * buses)))

    def hour(ahead, place):
        return neighbour(passed, ahead, (slice(None), slice(place * buses, (place + 1) * buses)))

    lev_front, bar_front = lone(True, 1), hour(True, 2)
    lev_behind, pow_behind, bar_behind = lone(False, 2), lone(False, 3), hour(False, 3)
    cap_new = capacity_of(hours, cap_ref, inv_ref, invest)
    capout_ref[...] = cap_new
    cap_bar = 2.0 * cap_new - cap_ref[...]
    rate = rr_ref[...]
    ramp_cap = rate * cap_bar
    cost = vc_ref[...]

    bal = bal_ref[...] + step_size * res_ref[...]
    bal2_ref[...] = bal
    lev_bar, pow_bar = levbar_ref[...], powbar_ref[...]
    shift_ref[8 : 8 + rows] = lev_bar
    shift_ref[8 + rows : 9 + rows] = lev_front
    sto = sto_ref[...] + step_size * (shift_ref[9 : 9 + rows] - lev_bar + pow_bar)
    sto2_ref[...] = sto
    sto_before = halo_ref[TECH : TECH + 1] + step_size * (
        levbar_ref[0:1] - lev_behind + pow_behind
    )
    shift_ref[8 : 8 + rows] = sto
    shift_ref[7:8] = sto_before
    ang_step = primal_step * (flow_ref[...] + step_size * resflow_ref[...])
    ang_old = ang_ref[...] + primal_step * flow_ref[...]
    ang2_ref[...] = ang_old + ang_step
    angbar2_ref[...] = ang_old + 2.0 * ang_step
    pow_old = pownew_ref[...]
    pow_new = pow_old - primal_step * (bal + sto)
    pow2_ref[...] = pow_new
    powbar2_ref[...] = 2.0 * pow_new - pow_old
    lev_old = levnew_ref[...]
    lev_new = jnp.maximum(0.0, lev_old - primal_step * (shift_ref[7 : 7 + rows] - sto))
    lev2_ref[...] = lev_new
    levbar2_ref[...] = 2.0 * lev_new - lev_old
    squares = add_squares(
        jnp.zeros((TECH, buses), F32), ang_step, pow_new - pow_old, lev_new - lev_old
    )

    unroll = divisor(rows, 7)

    def step(t, carry, first=False, last=False):
        bar, before, limit_sum, ramp_sum, squares = carry
        old = row_ref[...] if first else new_ref[t]
        bar_next = bar_front if last else bar_ref[t + 1]
        avail = avail_ref[t]
        lim = jnp.maximum(0.0, lim_ref[t] + step_size * (bar - avail * cap_bar))
        ramp = jnp.maximum(0.0, ramp_ref[t] + step_size * (bar_next - bar - ramp_cap))
        dual = jnp.broadcast_to(bal2_ref[pl.ds(t, 1), :], (TECH, buses))
        gen = jnp.maximum(0.0, old - primal_step * (cost + dual + lim + before - ramp))
        squares += (gen - old) ** 2
        limit_sum += avail * lim
        ramp_sum += ramp
        gen2_ref[t] = gen
        lim2_ref[t] = lim
        ramp2_ref[t] = ramp
        if first:
            out_ref[:, 2 * buses :] = 2.0 * gen - old
        return bar_next, ramp, limit_sum, ramp_sum, squares

    bar = mine_ref[:, 2 * buses : 3 * buses]
    before = jnp.maximum(0.0, halo_ref[:TECH] + step_size * (bar - bar_behind - ramp_cap))
    zero = jnp.zeros((TECH, buses), F32)
    carry = (bar, before, zero, zero, squares)
    for t in range(unroll):
        carry = step(t, carry, first=t == 0)

    def several(j, carry):
        for k in range(unroll):
            carry = step(j * unroll + k, carry)
        return carry

    carry = lax.fori_loop(1, rows // unroll - 1, several, carry)
    for t in range(rows - unroll, rows):
        carry = step(t, carry, last=t == rows - 1)
    _, _, limit_sum, ramp_sum, squares = carry
    put_totals(out_ref, limit_sum + rate * ramp_sum, squares, (levbar2_ref[0:1],), ())


def residual_two_body(
    pieces, gen_ref, ang_ref, lev_ref, pow_ref, new_ref, row_ref, powbar_ref, load_ref, high_ref, low_ref, *refs,
):
    sources, refs = refs[:pieces], refs[pieces:]
    out_ref, bar_ref, gen_h, ang_h, lev_h, pow_h, sum_ref, sems = refs
    copies = [
        pltpu.make_async_copy(source, target, sems.at[k])
        for k, (source, target) in enumerate(
            ((gen_ref, gen_h), (ang_ref, ang_h), (lev_ref, lev_h), (pow_ref, pow_h))
        )
    ]
    for copy in copies:
        copy.start()
    rows, _, buses = gen_ref.shape
    unroll = divisor(rows, 7)
    flow = network_product(sources, high_ref, low_ref)

    def one(t, old):
        bar = 2.0 * gen_ref[t] - old
        bar_ref[t] = bar
        sum_ref[pl.ds(t, 1), :] = jnp.sum(bar, axis=0, keepdims=True)

    for t in range(unroll):
        one(t, new_ref[t] if t else row_ref[...])

    def several(j, _):
        for k in range(unroll):
            one(j * unroll + k, new_ref[j * unroll + k])
        return 0

    lax.fori_loop(1, rows // unroll, several, 0)
    out_ref[...] = sum_ref[...] + powbar_ref[...] - flow - load_ref[...]
    for copy in copies:
        copy.wait()


def last_body(
    hours, entries, steps, here_ref, squares_ref, other_ref, *refs,
):
    passed, refs = refs[:steps], refs[steps:]
    (
        cap_ref, inv_ref, rr_ref,
        bar_ref, lim_ref, ramp_ref, avail_ref, bal_ref, res_ref, sto_ref, levbar_ref, powbar_ref,
        capout_ref, lim_h, ramp_h, balout_ref, stoout_ref, lim_v, ramp_v, shift_ref, sems,
    ) = refs
    rows, _, buses = bar_ref.shape
    chunk = divisor(rows, 28)
    unroll = divisor(chunk, 7)
    chunks = rows // chunk
    invest, step_size = get_totals(entries, buses, here_ref, squares_ref, other_ref)
    lev_front = neighbour(passed, True, (slice(1, 2), slice(buses, 2 * buses)))
    bar_front = neighbour(passed, True, (slice(None), slice(2 * buses, 3 * buses)))
    cap_new = capacity_of(hours, cap_ref, inv_ref, invest)
    capout_ref[...] = cap_new
    cap_bar = 2.0 * cap_new - cap_ref[...]
    ramp_cap = rr_ref[...] * cap_bar

    def copies(i):
        rows_here = pl.ds(i * chunk, chunk)
        return [
            pltpu.make_async_copy(source.at[rows_here], target.at[rows_here], sems.at[i, k])
            for k, (source, target) in enumerate(((lim_v, lim_h), (ramp_v, ramp_h)))
        ]

    def step(t, bar, last=False):
        bar_next = bar_front if last else bar_ref[t + 1]
        lim_v[t] = jnp.maximum(0.0, lim_ref[t] + step_size * (bar - avail_ref[t] * cap_bar))
        ramp_v[t] = jnp.maximum(0.0, ramp_ref[t] + step_size * (bar_next - bar - ramp_cap))
        return bar_next

    bar = bar_ref[0]
    for i in range(chunks):
        end = (i + 1) * chunk
        stop = end - unroll if i == chunks - 1 else end

        def several(j, bar, start=i * chunk):
            for k in range(unroll):
                bar = step(start + j * unroll + k, bar)
            return bar

        bar = lax.fori_loop(0, (stop - i * chunk) // unroll, several, bar)
        for t in range(stop, end):
            bar = step(t, bar, last=t == rows - 1)
        for copy in copies(i):
            copy.start()
    balout_ref[...] = bal_ref[...] + step_size * res_ref[...]
    lev_bar = levbar_ref[...]
    shift_ref[8 : 8 + rows] = lev_bar
    shift_ref[8 + rows : 9 + rows] = lev_front
    stoout_ref[...] = sto_ref[...] + step_size * (shift_ref[9 : 9 + rows] - lev_bar + powbar_ref[...])
    for i in range(chunks):
        for copy in copies(i):
            copy.wait()


def per_device(
    demand,
    avail_factor,
    tech_mask,
    var_cost,
    inv_cost,
    ramp_rate,
    network,
    pattern,
    live_hours,
    generation,
    angles,
    levels,
    net_power,
    capacity,
    balance_dual,
    storage_dual,
    limit_dual,
    ramp_dual,
):
    rows, buses = demand.shape
    hours = rows * lax.axis_size("hour")
    entries = float(hours * (TECH + 3) * BUS)
    swap = lax.axis_size("region") == 2
    pieces = 2 if swap else 1
    cube, flat, tech = (rows, TECH, buses), (rows, buses), (TECH, buses)
    shift = pltpu.VMEM((rows + 24, buses), F32)
    chunks = rows // divisor(rows, 28)

    def all_buses(block):
        if swap:
            return block, partner(block, "region", 1)
        return (lax.all_gather(block, "region", axis=1, tiled=True),)

    steps = len(distances("hour"))

    def totals(block, *work):
        row = lax.broadcasted_iota(jnp.int32, block.shape, 0)
        lane = lax.broadcasted_iota(jnp.int32, block.shape, 1)
        adds = (lane < buses) | ((lane < 2 * buses) & (row == 0))
        passed = []
        for k, distance in enumerate(distances("hour")):
            got = partner(block, "hour", distance)
            passed.append(got)
            if k < len(work) and work[k]:
                block = after(block, work[k]())
            block = got + jnp.where(adds, block, 0.0)
        squares = block
        *inner, outer = distances("region")
        for distance in inner:
            squares = squares + partner(squares, "region", distance)
        return block, squares, partner(squares, "region", outer), passed

    halo = jnp.concatenate(
        [ramp_dual[-1], jnp.broadcast_to(storage_dual[-1:], (TECH, buses))], axis=0
    )
    halo = shifted(halo, "hour", 1)
    balances = all_buses(balance_dual)

    bar, new, lim, ramp, avail, high, low, invest, square, load = call(
        functools.partial(load_body, swap),
        (generation, limit_dual, ramp_dual, avail_factor, network, tech_mask, var_cost, ramp_rate,
         balance_dual, demand, pattern, live_hours),
        [HBM] * 11 + [SMEM],
        [(cube, F32)] * 5 + [((buses, BUS), jnp.bfloat16)] * 2 + [(tech, F32)] * 2 + [(flat, F32)],
        scratch=(
            pltpu.VMEM(cube, jnp.bfloat16),
            pltpu.VMEM((buses, BUS), F32),
            pltpu.VMEM(tech, jnp.int32),
            pltpu.VMEM(tech, F32),
            pltpu.VMEM(tech, F32),
            pltpu.VMEM(flat, F32),
            pltpu.VMEM(flat, F32),
            pltpu.SMEM(pattern.shape, jnp.int32),
            pltpu.SemaphoreType.DMA((chunks, 4)),
            pltpu.SemaphoreType.DMA((pieces,)),
            pltpu.SemaphoreType.DMA((6,)),
        ),
        name="load",
    )
    (
        row, flow, ang_bar, pow_new, pow_bar, lev_new, lev_bar, total,
    ) = call(
        functools.partial(first_body, pieces),
        (bar, lim, ramp, halo, var_cost, invest, square, balance_dual, *balances,
         angles, net_power, levels, storage_dual, high, low),
        [VMEM] * (8 + pieces + 6),
        [(tech, F32)] + [(flat, F32)] * 6 + [((TECH, 4 * buses), F32)],
        scratch=(shift,),
        name="first",
    )
    sources = all_buses(ang_bar)
    made = {}

    def residual():
        (made["res"],) = call(
            functools.partial(residual_one_body, pieces),
            (bar, total, pow_bar, load, high, low, *sources),
            [VMEM] * (6 + pieces),
            [(flat, F32)],
            scratch=(pltpu.VMEM(flat, F32),),
            name="residual1",
        )
        return made["res"]

    def product():
        (made["flow"],) = call(
            functools.partial(product_body, pieces),
            (high, low, *all_buses(made["res"])),
            [VMEM] * (2 + pieces),
            [(flat, F32)],
            name="product",
        )
        return made["flow"]

    here, squares, other, passed = totals(total, None, residual, None, product)
    res, res_flow = made["res"], made["flow"]
    (
        cap, gen2, lim1, ramp1, bal1, sto1, ang2, ang_bar2, pow2, pow_bar2, lev2, lev_bar2, total2,
    ) = call(
        functools.partial(middle_body, hours, entries, steps),
        (here, squares, other, total, *passed, capacity, inv_cost, ramp_rate, var_cost, bar, new, row, lim, ramp, avail,
         halo, balance_dual, res, res_flow, flow, angles, pow_new, pow_bar, lev_new, lev_bar,
         storage_dual),
        [VMEM] * (25 + steps),
        [(tech, F32)] + [(cube, F32)] * 3 + [(flat, F32)] * 8 + [((TECH, 3 * buses), F32)],
        scratch=(shift,),
        name="middle",
    )
    sources2 = all_buses(ang_bar2)

    def residual2():
        made["two"] = call(
            functools.partial(residual_two_body, pieces),
            (gen2, ang2, lev2, pow2, new, row, pow_bar2, load, high, low, *sources2),
            [VMEM] * (10 + pieces),
            [(flat, F32), (cube, F32), (cube, F32)] + [(flat, F32)] * 3,
            out_specs=[VMEM] * 2 + [HBM] * 4,
            scratch=(pltpu.VMEM(flat, F32), pltpu.SemaphoreType.DMA((4,))),
            name="residual2",
        )
        return made["two"][0]

    here2, squares2, other2, passed2 = totals(total2, None, residual2)
    res2, bar2, gen2, ang2, lev2, pow2 = made["two"]
    cap2, lim2, ramp2, bal2, sto2 = call(
        functools.partial(last_body, hours, entries, steps),
        (here2, squares2, other2, *passed2, cap, inv_cost, ramp_rate, bar2, lim1, ramp1, avail, bal1, res2, sto1,
         lev_bar2, pow_bar2),
        [VMEM] * (15 + steps),
        [(tech, F32), (cube, F32), (cube, F32), (flat, F32), (flat, F32)],
        out_specs=[VMEM, HBM, HBM, VMEM, VMEM],
        scratch=(
            pltpu.VMEM(cube, F32), pltpu.VMEM(cube, F32), shift, pltpu.SemaphoreType.DMA((chunks, 2)),
        ),
        name="last",
    )
    return gen2, ang2, lev2, pow2, cap2, bal2, sto2, lim2, ramp2


def solution(mesh):
    return jax.shard_map(
        per_device,
        mesh=mesh,
        in_specs=(
            P("hour", "region"),
            P("hour", None, "region"),
            P(None, "region"),
            P(None, "region"),
            P(None, "region"),
            P(None, "region"),
            P("region", None),
            P(),
            P(),
            P("hour", None, "region"),
            P("hour", "region"),
            P("hour", "region"),
            P("hour", "region"),
            P(None, "region"),
            P("hour", "region"),
            P("hour", "region"),
            P("hour", None, "region"),
            P("hour", None, "region"),
        ),
        out_specs=(
            P("hour", None, "region"),
            P("hour", "region"),
            P("hour", "region"),
            P("hour", "region"),
            P(None, "region"),
            P("hour", "region"),
            P("hour", "region"),
            P("hour", None, "region"),
            P("hour", None, "region"),
        ),
        check_vma=False,
    )
```

```python
import functools

import jax
import jax.numpy as jnp
from jax import lax
from jax.experimental import pallas as pl
from jax.experimental.pallas import tpu as pltpu
from jax.sharding import PartitionSpec as P

BUS = 1024
TECH = 8
BLOCK = 128
ITERS = 2

primal_step = 0.2
capacity_step = 4.0
dual_scale = 0.06

F32 = jnp.float32
VMEM = pl.BlockSpec(memory_space=pltpu.VMEM)
SMEM = pl.BlockSpec(memory_space=pltpu.SMEM)
HBM = pl.BlockSpec(memory_space=pltpu.HBM)


def shifted(block, axis, distance):
    devices = range(lax.axis_size(axis))
    route = [((i - distance) % len(devices), i) for i in devices]
    return lax.ppermute(block, axis, route)


def partner(block, axis, distance):
    return lax.ppermute(block, axis, [(i, i ^ distance) for i in range(lax.axis_size(axis))])


def distances(axis):
    size = lax.axis_size(axis)
    return [1 << i for i in range(size.bit_length() - 1)]


def summed(block, axis):
    for distance in distances(axis):
        block = block + partner(block, axis, distance)
    return block


def after(block, earlier):
    return lax.optimization_barrier((block, earlier))[0]


def divisor(extent, most):
    return max(d for d in range(1, most + 1) if extent % d == 0)


def split(value):
    high = value.astype(jnp.bfloat16)
    return high, (value - high.astype(F32)).astype(jnp.bfloat16)


def network_product(sources, high_ref, low_ref):
    total, at = None, 0
    for source in sources:
        columns = slice(at, at + source.shape[1])
        at += source.shape[1]
        high, low = split(source[...])
        for left, right in ((high, high_ref), (low, high_ref), (high, low_ref)):
            term = lax.dot_general(
                left, right[:, columns], (((1,), (1,)), ((), ())), preferred_element_type=F32
            )
            total = term if total is None else total + term
    return total


def call(body, operands, specs, outs, out_specs=None, scratch=(), flops=1 << 22, moved=1 << 23, room=8, name=None):
    operands = [
        pltpu.with_memory_space_constraint(operand, pltpu.HBM) if spec is HBM else operand
        for operand, spec in zip(operands, specs)
    ]
    return pl.pallas_call(
        body,
        out_shape=[jax.ShapeDtypeStruct(shape, dtype) for shape, dtype in outs],
        in_specs=specs,
        out_specs=out_specs or [VMEM] * len(outs),
        scratch_shapes=list(scratch),
        compiler_params=pltpu.CompilerParams(vmem_limit_bytes=room << 20),
        cost_estimate=pl.CostEstimate(flops=flops, bytes_accessed=moved, transcendentals=0),
        name=name,
    )(*operands)


def pack_body(ramp_h, sto_h, *refs):
    halo_ref, sto_v, sems = refs[-3:]
    rows = ramp_h.shape[0]
    start = (rows - 1) // TECH * TECH
    copies = [
        pltpu.make_async_copy(ramp_h.at[rows - 1], halo_ref.at[pl.ds(0, TECH)], sems.at[0]),
        pltpu.make_async_copy(sto_h.at[pl.ds(start, rows - start)], sto_v, sems.at[1]),
    ]
    for copy in copies:
        copy.start()
    for copy in copies:
        copy.wait()
    halo_ref[TECH:] = jnp.broadcast_to(sto_v[rows - 1 - start : rows - start], (TECH, sto_v.shape[1]))


def load_body(
    swap, gen_ref, lim_ref, ramp_ref, av_ref, net_ref, mask_ref, vc_ref, rr_ref, bal_ref, demand_ref, pat_s, live_s,
    ang_ref, pow_ref, sto_ref, *refs,
):
    (
        bar_ref, new_ref, avail_ref, high_ref, low_ref, invest_ref, square_ref, load_ref,
        flow_ref, angbar_ref, pownew_ref, powbar_ref,
    ) = refs[-12:]
    others = refs[:-12]
    rows, _, buses = gen_ref.shape
    unroll = divisor(rows, 7)
    region = lax.axis_index("region")
    pieces = 2 if swap else 1
    width = BUS // pieces
    blocks = buses // BLOCK
    shift = region * blocks if swap else 0
    for i in range(blocks):
        for j in range(BUS // BLOCK):
            at = (slice(i * BLOCK, (i + 1) * BLOCK), slice(j * BLOCK, (j + 1) * BLOCK))
            place = lax.rem(j + shift, BUS // BLOCK)
            coupled = pat_s[region * blocks + i, place].astype(F32)
            source = net_ref[at[0], pl.ds(pl.multiple_of(place * BLOCK, BLOCK), BLOCK)]
            high, low = split(source * coupled)
            high_ref[at] = high
            low_ref[at] = low

    mask = mask_ref[...].astype(F32)
    cost = vc_ref[...]
    live = live_s[0] - lax.axis_index("hour") * rows

    def step(t, carry, first=False):
        before, limit_sum, ramp_sum, squares = carry
        gen, lim, ramp = gen_ref[t], lim_ref[t], ramp_ref[t]
        alive = jnp.where(t < live, 1.0, 0.0).astype(F32)
        avail = av_ref[t].astype(F32) * mask * alive
        avail_ref[t] = avail
        limit_sum += avail * lim
        ramp_sum += ramp
        if not first:
            dual = jnp.broadcast_to(bal_ref[pl.ds(t, 1), :], (TECH, buses))
            new = jnp.maximum(0.0, gen - primal_step * (cost + dual + lim + before - ramp))
            squares += (new - gen) ** 2
            new_ref[t] = new
            bar_ref[t] = 2.0 * new - gen
        else:
            bar_ref[t] = gen
        return ramp, limit_sum, ramp_sum, squares

    carry = (jnp.zeros((TECH, buses), F32),) * 4
    for t in range(unroll):
        carry = step(t, carry, t == 0)

    def several(j, carry):
        for k in range(unroll):
            carry = step(j * unroll + k, carry)
        return carry

    _, limit_sum, ramp_sum, squares = lax.fori_loop(1, rows // unroll, several, carry)
    invest_ref[...] = limit_sum + rr_ref[...] * ramp_sum
    flow = network_product(others, high_ref, low_ref)
    flow_ref[...] = flow
    ang_step = primal_step * flow
    angbar_ref[...] = ang_ref[...] + 2.0 * ang_step
    pow_old = pow_ref[...]
    pow_new = pow_old - primal_step * (bal_ref[...] + sto_ref[...])
    pownew_ref[...] = pow_new
    powbar_ref[...] = 2.0 * pow_new - pow_old
    square_ref[...] = add_squares(squares, ang_step, pow_new - pow_old)
    row = lax.broadcasted_iota(jnp.int32, (rows, buses), 0)
    load_ref[...] = jnp.where(row < live, demand_ref[...], 0.0)


def fold_rows(square):
    rows = square.shape[0]
    full = rows // TECH * TECH
    total = jnp.sum(square[:full].reshape(full // TECH, TECH, square.shape[1]), axis=0)
    return total, square[full:]


def layout(buses, lone):
    width = max(BLOCK, buses * (1 << (lone + 1).bit_length() - 1) // TECH)
    return width, buses // width


def put_totals(out_ref, lone, invest, squares, rows_of_one):
    buses = invest.shape[1]
    width, parts = layout(buses, lone)
    lanes = slice(buses, buses + width)
    out_ref[:, :buses] = invest
    out_ref[:, lanes] = jnp.zeros((TECH, width), F32)
    for i, row in enumerate((jnp.sum(squares, axis=0, keepdims=True), *rows_of_one)):
        for j in range(parts):
            out_ref[i * parts + j : i * parts + j + 1, lanes] = row[:, j * width : (j + 1) * width]


def put_cubes(out_ref, lone, *cubes):
    start = cubes[0].shape[1] + layout(cubes[0].shape[1], lone)[0]
    for i, cube in enumerate(cubes):
        out_ref[:, start + i * cube.shape[1] : start + (i + 1) * cube.shape[1]] = cube


def get_totals(entries, buses, lone, here_ref, squares_ref, other_ref):
    width, parts = layout(buses, lone)
    at = (slice(0, parts), slice(buses, buses + width))
    squares = jnp.sum(squares_ref[at] + other_ref[at])
    return here_ref[:, :buses], dual_scale * lax.rsqrt(jnp.full((1, 1), squares / entries + 1e-06, F32))


def get_row(buses, lone, index, read):
    width, parts = layout(buses, lone)
    lanes = slice(buses, buses + width)
    return jnp.concatenate(
        [read((slice(i, i + 1), lanes)) for i in range(index * parts, (index + 1) * parts)], axis=1
    )


def get_cube(buses, lone, index, read):
    start = buses + layout(buses, lone)[0] + index * buses
    return read((slice(None), slice(start, start + buses)))


def neighbour(passed, ahead, index):
    device = lax.axis_index("hour")
    block = passed[0][index]
    for k in range(1, len(passed)):
        low = lax.rem(device, 1 << k)
        differs = low == (1 << k) - 1 if ahead else low == 0
        block = jnp.where(differs, passed[k][index], block)
    return block


def add_squares(total, *terms):
    for term in terms:
        full, rest = fold_rows(term * term)
        total = total + full
        if rest.shape[0]:
            rest = jnp.sum(rest, axis=0, keepdims=True)
            row = lax.broadcasted_iota(jnp.int32, total.shape, 0)
            total = total + jnp.where(row == 0, rest, 0.0)
    return total


def first_body(
    bar_ref, lim_ref, ramp_ref, halo_ref, vc_ref, invest_ref, square_ref, bal_ref, lev_ref, sto_ref, powbar_ref,
    row_ref, levnew_ref, levbar_ref, total_ref, shift_ref,
):
    rows, _, buses = bar_ref.shape
    gen = bar_ref[0]
    dual = jnp.broadcast_to(bal_ref[0:1, :], (TECH, buses))
    new = jnp.maximum(
        0.0, gen - primal_step * (vc_ref[...] + dual + lim_ref[0] + halo_ref[:TECH] - ramp_ref[0])
    )
    row_ref[...] = new
    sto = sto_ref[...]
    shift_ref[8 : 8 + rows] = sto
    shift_ref[7:8] = halo_ref[TECH : TECH + 1]
    lev_old = lev_ref[...]
    lev_new = jnp.maximum(0.0, lev_old - primal_step * (shift_ref[7 : 7 + rows] - sto))
    levnew_ref[...] = lev_new
    levbar_ref[...] = 2.0 * lev_new - lev_old
    put_totals(
        total_ref, 3, invest_ref[...], add_squares(square_ref[...], new - gen, lev_new - lev_old),
        (levbar_ref[0:1], levbar_ref[rows - 1 : rows], powbar_ref[rows - 1 : rows]),
    )
    put_cubes(total_ref, 3, 2.0 * new - gen, bar_ref[rows - 1])


def residual_one_body(
    pieces, bar_ref, total_ref, powbar_ref, load_ref, high_ref, low_ref, *refs,
):
    sources, (out_ref, sum_ref) = refs[:pieces], refs[pieces:]
    rows, _, buses = bar_ref.shape
    unroll = divisor(rows, 7)
    flow = network_product(sources, high_ref, low_ref)

    def several(j, _):
        for k in range(unroll):
            t = j * unroll + k
            sum_ref[pl.ds(t, 1), :] = jnp.sum(bar_ref[t], axis=0, keepdims=True)
        return 0

    lax.fori_loop(0, rows // unroll, several, 0)
    bar = get_cube(buses, 3, 0, total_ref.__getitem__)
    sum_ref[0:1] = jnp.sum(bar, axis=0, keepdims=True)
    out_ref[...] = sum_ref[...] + powbar_ref[...] - flow - load_ref[...]


def product_body(pieces, high_ref, low_ref, *refs):
    refs[pieces][...] = network_product(refs[:pieces], high_ref, low_ref)


def capacity_of(hours, cap_ref, inv_ref, invest):
    return jnp.maximum(0.0, cap_ref[...] - capacity_step * (inv_ref[...] - invest / float(hours)))


def middle_body(
    hours, entries, steps, here_ref, squares_ref, other_ref, mine_ref, *refs,
):
    passed, refs = refs[:steps], refs[steps:]
    (
        cap_ref, inv_ref, rr_ref, vc_ref,
        bar_ref, new_ref, row_ref, lim_ref, ramp_ref, avail_ref, halo_ref,
        bal_ref, res_ref, resflow_ref, flow_ref, ang_ref, pownew_ref, powbar_ref, levnew_ref, levbar_ref, sto_ref,
        capout_ref, gen2_ref, lim2_ref, ramp2_ref, bal2_ref, sto2_ref, ang2_ref, angbar2_ref, pow2_ref,
        powbar2_ref, lev2_ref, levbar2_ref, out_ref, shift_ref,
    ) = refs
    rows, _, buses = bar_ref.shape
    invest, step_size = get_totals(entries, buses, 3, here_ref, squares_ref, other_ref)
    from_next = functools.partial(neighbour, passed, True)
    from_last = functools.partial(neighbour, passed, False)
    lev_front = get_row(buses, 3, 1, from_next)
    bar_front = get_cube(buses, 3, 0, from_next)
    lev_behind = get_row(buses, 3, 2, from_last)
    pow_behind = get_row(buses, 3, 3, from_last)
    bar_behind = get_cube(buses, 3, 1, from_last)
    cap_new = capacity_of(hours, cap_ref, inv_ref, invest)
    capout_ref[...] = cap_new
    cap_bar = 2.0 * cap_new - cap_ref[...]
    rate = rr_ref[...]
    ramp_cap = rate * cap_bar
    cost = vc_ref[...]

    bal = bal_ref[...] + step_size * res_ref[...]
    bal2_ref[...] = bal
    lev_bar, pow_bar = levbar_ref[...], powbar_ref[...]
    shift_ref[8 : 8 + rows] = lev_bar
    shift_ref[8 + rows : 9 + rows] = lev_front
    sto = sto_ref[...] + step_size * (shift_ref[9 : 9 + rows] - lev_bar + pow_bar)
    sto2_ref[...] = sto
    sto_before = halo_ref[TECH : TECH + 1] + step_size * (
        levbar_ref[0:1] - lev_behind + pow_behind
    )
    shift_ref[8 : 8 + rows] = sto
    shift_ref[7:8] = sto_before
    ang_step = primal_step * (flow_ref[...] + step_size * resflow_ref[...])
    ang_old = ang_ref[...] + primal_step * flow_ref[...]
    ang2_ref[...] = ang_old + ang_step
    angbar2_ref[...] = ang_old + 2.0 * ang_step
    pow_old = pownew_ref[...]
    pow_new = pow_old - primal_step * (bal + sto)
    pow2_ref[...] = pow_new
    powbar2_ref[...] = 2.0 * pow_new - pow_old
    lev_old = levnew_ref[...]
    lev_new = jnp.maximum(0.0, lev_old - primal_step * (shift_ref[7 : 7 + rows] - sto))
    lev2_ref[...] = lev_new
    levbar2_ref[...] = 2.0 * lev_new - lev_old
    squares = add_squares(
        jnp.zeros((TECH, buses), F32), ang_step, pow_new - pow_old, lev_new - lev_old
    )

    unroll = divisor(rows, 7)

    def step(t, carry, first=False, last=False):
        bar, before, limit_sum, ramp_sum, squares = carry
        old = row_ref[...] if first else new_ref[t]
        bar_next = bar_front if last else bar_ref[t + 1]
        avail = avail_ref[t]
        lim = jnp.maximum(0.0, lim_ref[t] + step_size * (bar - avail * cap_bar))
        ramp = jnp.maximum(0.0, ramp_ref[t] + step_size * (bar_next - bar - ramp_cap))
        dual = jnp.broadcast_to(bal2_ref[pl.ds(t, 1), :], (TECH, buses))
        gen = jnp.maximum(0.0, old - primal_step * (cost + dual + lim + before - ramp))
        squares += (gen - old) ** 2
        limit_sum += avail * lim
        ramp_sum += ramp
        gen2_ref[t] = gen
        lim2_ref[t] = lim
        ramp2_ref[t] = ramp
        if first:
            put_cubes(out_ref, 1, 2.0 * gen - old)
        return bar_next, ramp, limit_sum, ramp_sum, squares

    bar = get_cube(buses, 3, 0, mine_ref.__getitem__)
    before = jnp.maximum(0.0, halo_ref[:TECH] + step_size * (bar - bar_behind - ramp_cap))
    zero = jnp.zeros((TECH, buses), F32)
    carry = (bar, before, zero, zero, squares)
    for t in range(unroll):
        carry = step(t, carry, first=t == 0)

    def several(j, carry):
        for k in range(unroll):
            carry = step(j * unroll + k, carry)
        return carry

    carry = lax.fori_loop(1, rows // unroll - 1, several, carry)
    for t in range(rows - unroll, rows):
        carry = step(t, carry, last=t == rows - 1)
    _, _, limit_sum, ramp_sum, squares = carry
    put_totals(out_ref, 1, limit_sum + rate * ramp_sum, squares, (levbar2_ref[0:1],))


def residual_two_body(
    pieces, gen_ref, ang_ref, lev_ref, pow_ref, new_ref, row_ref, powbar_ref, load_ref, high_ref, low_ref, *refs,
):
    sources, refs = refs[:pieces], refs[pieces:]
    out_ref, bar_ref, gen_h, ang_h, lev_h, pow_h, sum_ref, sems = refs
    copies = [
        pltpu.make_async_copy(source, target, sems.at[k])
        for k, (source, target) in enumerate(
            ((gen_ref, gen_h), (ang_ref, ang_h), (lev_ref, lev_h), (pow_ref, pow_h))
        )
    ]
    for copy in copies:
        copy.start()
    rows, _, buses = gen_ref.shape
    unroll = divisor(rows, 7)
    flow = network_product(sources, high_ref, low_ref)

    def one(t, old):
        bar = 2.0 * gen_ref[t] - old
        bar_ref[t] = bar
        sum_ref[pl.ds(t, 1), :] = jnp.sum(bar, axis=0, keepdims=True)

    for t in range(unroll):
        one(t, new_ref[t] if t else row_ref[...])

    def several(j, _):
        for k in range(unroll):
            one(j * unroll + k, new_ref[j * unroll + k])
        return 0

    lax.fori_loop(1, rows // unroll, several, 0)
    out_ref[...] = sum_ref[...] + powbar_ref[...] - flow - load_ref[...]
    for copy in copies:
        copy.wait()


def last_body(
    hours, entries, steps, here_ref, squares_ref, other_ref, *refs,
):
    passed, refs = refs[:steps], refs[steps:]
    (
        cap_ref, inv_ref, rr_ref,
        bar_ref, lim_ref, ramp_ref, avail_ref, bal_ref, res_ref, sto_ref, levbar_ref, powbar_ref,
        capout_ref, lim_h, ramp_h, balout_ref, stoout_ref, lim_v, ramp_v, shift_ref, sems,
    ) = refs
    rows, _, buses = bar_ref.shape
    chunk = divisor(rows, 28)
    unroll = divisor(chunk, 7)
    chunks = rows // chunk
    invest, step_size = get_totals(entries, buses, 1, here_ref, squares_ref, other_ref)
    from_next = functools.partial(neighbour, passed, True)
    lev_front = get_row(buses, 1, 1, from_next)
    bar_front = get_cube(buses, 1, 0, from_next)
    cap_new = capacity_of(hours, cap_ref, inv_ref, invest)
    capout_ref[...] = cap_new
    cap_bar = 2.0 * cap_new - cap_ref[...]
    ramp_cap = rr_ref[...] * cap_bar

    def copies(i):
        rows_here = pl.ds(i * chunk, chunk)
        return [
            pltpu.make_async_copy(source.at[rows_here], target.at[rows_here], sems.at[i, k])
            for k, (source, target) in enumerate(((lim_v, lim_h), (ramp_v, ramp_h)))
        ]

    def step(t, bar, last=False):
        bar_next = bar_front if last else bar_ref[t + 1]
        lim_v[t] = jnp.maximum(0.0, lim_ref[t] + step_size * (bar - avail_ref[t] * cap_bar))
        ramp_v[t] = jnp.maximum(0.0, ramp_ref[t] + step_size * (bar_next - bar - ramp_cap))
        return bar_next

    bar = bar_ref[0]
    for i in range(chunks):
        end = (i + 1) * chunk
        stop = end - unroll if i == chunks - 1 else end

        def several(j, bar, start=i * chunk):
            for k in range(unroll):
                bar = step(start + j * unroll + k, bar)
            return bar

        bar = lax.fori_loop(0, (stop - i * chunk) // unroll, several, bar)
        for t in range(stop, end):
            bar = step(t, bar, last=t == rows - 1)
        for copy in copies(i):
            copy.start()
    balout_ref[...] = bal_ref[...] + step_size * res_ref[...]
    lev_bar = levbar_ref[...]
    shift_ref[8 : 8 + rows] = lev_bar
    shift_ref[8 + rows : 9 + rows] = lev_front
    stoout_ref[...] = sto_ref[...] + step_size * (shift_ref[9 : 9 + rows] - lev_bar + powbar_ref[...])
    for i in range(chunks):
        for copy in copies(i):
            copy.wait()


def per_device(
    demand,
    avail_factor,
    tech_mask,
    var_cost,
    inv_cost,
    ramp_rate,
    network,
    pattern,
    live_hours,
    generation,
    angles,
    levels,
    net_power,
    capacity,
    balance_dual,
    storage_dual,
    limit_dual,
    ramp_dual,
):
    rows, buses = demand.shape
    hours = rows * lax.axis_size("hour")
    entries = float(hours * (TECH + 3) * BUS)
    swap = lax.axis_size("region") == 2
    pieces = 2 if swap else 1
    cube, flat, tech = (rows, TECH, buses), (rows, buses), (TECH, buses)
    shift = pltpu.VMEM((rows + 24, buses), F32)
    chunks = rows // divisor(rows, 28)

    def all_buses(block):
        if swap:
            return block, partner(block, "region", 1)
        return (lax.all_gather(block, "region", axis=1, tiled=True),)

    steps = len(distances("hour"))

    def totals(block, lone, *work):
        row = lax.broadcasted_iota(jnp.int32, block.shape, 0)
        lane = lax.broadcasted_iota(jnp.int32, block.shape, 1)
        width, parts = layout(buses, lone)
        adds = (lane < buses) | ((lane < buses + width) & (row < parts))
        passed = []
        for k, distance in enumerate(distances("hour")):
            got = partner(block, "hour", distance)
            passed.append(got)
            if k < len(work) and work[k]:
                block = after(block, work[k]())
            block = got + jnp.where(adds, block, 0.0)
        squares = block
        *inner, outer = distances("region")
        for distance in inner:
            squares = squares + partner(squares, "region", distance)
        return block, squares, partner(squares, "region", outer), passed

    (halo,) = call(
        pack_body,
        (ramp_dual, storage_dual, generation, limit_dual, network, avail_factor, demand, tech_mask,
         angles, net_power, levels),
        [HBM] * 11,
        [((2 * TECH, buses), F32)],
        scratch=(pltpu.VMEM((rows - (rows - 1) // TECH * TECH, buses), F32), pltpu.SemaphoreType.DMA((2,))),
        moved=1 << 28,
        name="pack",
    )
    balances = all_buses(after(balance_dual, halo))
    halo = shifted(halo, "hour", 1)

    bar, new, avail, high, low, invest, square, load, flow, ang_bar, pow_new, pow_bar = call(
        functools.partial(load_body, swap),
        (generation, limit_dual, ramp_dual, avail_factor, network, tech_mask, var_cost, ramp_rate,
         balance_dual, demand, pattern, live_hours, angles, net_power, storage_dual, *balances),
        [VMEM] * 10 + [SMEM] * 2 + [VMEM] * (3 + pieces),
        [(cube, F32)] * 3 + [((buses, BUS), jnp.bfloat16)] * 2 + [(tech, F32)] * 2 + [(flat, F32)] * 5,
        name="load",
    )
    lim, ramp = limit_dual, ramp_dual
    row, lev_new, lev_bar, total = call(
        first_body,
        (bar, lim, ramp, halo, var_cost, invest, square, balance_dual, levels, storage_dual, pow_bar),
        [VMEM] * 11,
        [(tech, F32)] + [(flat, F32)] * 2 + [((TECH, 3 * buses + layout(buses, 3)[0]), F32)],
        scratch=(shift,),
        name="first",
    )
    sources = all_buses(ang_bar)
    made = {}

    def residual():
        (made["res"],) = call(
            functools.partial(residual_one_body, pieces),
            (bar, total, pow_bar, load, high, low, *sources),
            [VMEM] * (6 + pieces),
            [(flat, F32)],
            scratch=(pltpu.VMEM(flat, F32),),
            name="residual1",
        )
        return made["res"]

    def product():
        (made["flow"],) = call(
            functools.partial(product_body, pieces),
            (high, low, *all_buses(made["res"])),
            [VMEM] * (2 + pieces),
            [(flat, F32)],
            name="product",
        )
        return made["flow"]

    here, squares, other, passed = totals(total, 3, None, residual, None, product)
    res, res_flow = made["res"], made["flow"]
    (
        cap, gen2, lim1, ramp1, bal1, sto1, ang2, ang_bar2, pow2, pow_bar2, lev2, lev_bar2, total2,
    ) = call(
        functools.partial(middle_body, hours, entries, steps),
        (here, squares, other, total, *passed, capacity, inv_cost, ramp_rate, var_cost, bar, new, row, lim, ramp, avail,
         halo, balance_dual, res, res_flow, flow, angles, pow_new, pow_bar, lev_new, lev_bar,
         storage_dual),
        [VMEM] * (25 + steps),
        [(tech, F32)] + [(cube, F32)] * 3 + [(flat, F32)] * 8 + [((TECH, 2 * buses + layout(buses, 1)[0]), F32)],
        scratch=(shift,),
        name="middle",
    )
    sources2 = all_buses(ang_bar2)

    def residual2():
        made["two"] = call(
            functools.partial(residual_two_body, pieces),
            (gen2, ang2, lev2, pow2, new, row, pow_bar2, load, high, low, *sources2),
            [VMEM] * (10 + pieces),
            [(flat, F32), (cube, F32), (cube, F32)] + [(flat, F32)] * 3,
            out_specs=[VMEM] * 2 + [HBM] * 4,
            scratch=(pltpu.VMEM(flat, F32), pltpu.SemaphoreType.DMA((4,))),
            name="residual2",
        )
        return made["two"][0]

    here2, squares2, other2, passed2 = totals(total2, 1, None, residual2)
    res2, bar2, gen2, ang2, lev2, pow2 = made["two"]
    cap2, lim2, ramp2, bal2, sto2 = call(
        functools.partial(last_body, hours, entries, steps),
        (here2, squares2, other2, *passed2, cap, inv_cost, ramp_rate, bar2, lim1, ramp1, avail, bal1, res2, sto1,
         lev_bar2, pow_bar2),
        [VMEM] * (15 + steps),
        [(tech, F32), (cube, F32), (cube, F32), (flat, F32), (flat, F32)],
        out_specs=[VMEM, HBM, HBM, VMEM, VMEM],
        scratch=(
            pltpu.VMEM(cube, F32), pltpu.VMEM(cube, F32), shift, pltpu.SemaphoreType.DMA((chunks, 2)),
        ),
        name="last",
    )
    return gen2, ang2, lev2, pow2, cap2, bal2, sto2, lim2, ramp2


def solution(mesh):
    return jax.shard_map(
        per_device,
        mesh=mesh,
        in_specs=(
            P("hour", "region"),
            P("hour", None, "region"),
            P(None, "region"),
            P(None, "region"),
            P(None, "region"),
            P(None, "region"),
            P("region", None),
            P(),
            P(),
            P("hour", None, "region"),
            P("hour", "region"),
            P("hour", "region"),
            P("hour", "region"),
            P(None, "region"),
            P("hour", "region"),
            P("hour", "region"),
            P("hour", None, "region"),
            P("hour", None, "region"),
        ),
        out_specs=(
            P("hour", None, "region"),
            P("hour", "region"),
            P("hour", "region"),
            P("hour", "region"),
            P(None, "region"),
            P("hour", "region"),
            P("hour", "region"),
            P("hour", None, "region"),
            P("hour", None, "region"),
        ),
        check_vma=False,
    )
```

```python
import functools

import jax
import jax.numpy as jnp
from jax import lax
from jax.experimental import pallas as pl
from jax.experimental.pallas import tpu as pltpu
from jax.sharding import PartitionSpec as P

BUS = 1024
TECH = 8
BLOCK = 128
ITERS = 2

primal_step = 0.2
capacity_step = 4.0
dual_scale = 0.06

F32 = jnp.float32
VMEM = pl.BlockSpec(memory_space=pltpu.VMEM)
SMEM = pl.BlockSpec(memory_space=pltpu.SMEM)
HBM = pl.BlockSpec(memory_space=pltpu.HBM)


def shifted(block, axis, distance):
    devices = range(lax.axis_size(axis))
    route = [((i - distance) % len(devices), i) for i in devices]
    return lax.ppermute(block, axis, route)


def partner(block, axis, distance):
    return lax.ppermute(block, axis, [(i, i ^ distance) for i in range(lax.axis_size(axis))])


def distances(axis):
    size = lax.axis_size(axis)
    return [1 << i for i in range(size.bit_length() - 1)]


def summed(block, axis):
    for distance in distances(axis):
        block = block + partner(block, axis, distance)
    return block


def after(block, earlier):
    return lax.optimization_barrier((block, earlier))[0]


def divisor(extent, most):
    return max(d for d in range(1, most + 1) if extent % d == 0)


def split(value):
    high = value.astype(jnp.bfloat16)
    return high, (value - high.astype(F32)).astype(jnp.bfloat16)


def network_product(sources, high_ref, low_ref):
    total, at = None, 0
    for source in sources:
        columns = slice(at, at + source.shape[1])
        at += source.shape[1]
        high, low = split(source[...])
        for left, right in ((high, high_ref), (low, high_ref), (high, low_ref)):
            term = lax.dot_general(
                left, right[:, columns], (((1,), (1,)), ((), ())), preferred_element_type=F32
            )
            total = term if total is None else total + term
    return total


def call(body, operands, specs, outs, out_specs=None, scratch=(), flops=1 << 22, moved=1 << 23, room=8, name=None):
    operands = [
        pltpu.with_memory_space_constraint(operand, pltpu.HBM) if spec is HBM else operand
        for operand, spec in zip(operands, specs)
    ]
    return pl.pallas_call(
        body,
        out_shape=[jax.ShapeDtypeStruct(shape, dtype) for shape, dtype in outs],
        in_specs=specs,
        out_specs=out_specs or [VMEM] * len(outs),
        scratch_shapes=list(scratch),
        compiler_params=pltpu.CompilerParams(vmem_limit_bytes=room << 20),
        cost_estimate=pl.CostEstimate(flops=flops, bytes_accessed=moved, transcendentals=0),
        name=name,
    )(*operands)


def pack_body(ramp_h, sto_h, *refs):
    halo_ref, sto_v, sems = refs[-3:]
    rows = ramp_h.shape[0]
    start = (rows - 1) // TECH * TECH
    copies = [
        pltpu.make_async_copy(ramp_h.at[rows - 1], halo_ref.at[pl.ds(0, TECH)], sems.at[0]),
        pltpu.make_async_copy(sto_h.at[pl.ds(start, rows - start)], sto_v, sems.at[1]),
    ]
    for copy in copies:
        copy.start()
    for copy in copies:
        copy.wait()
    halo_ref[TECH:] = jnp.broadcast_to(sto_v[rows - 1 - start : rows - start], (TECH, sto_v.shape[1]))


def load_body(
    swap, gen_ref, lim_ref, ramp_ref, av_ref, net_ref, mask_ref, vc_ref, rr_ref, bal_ref, demand_ref, pat_s, live_s,
    ang_ref, pow_ref, sto_ref, *refs,
):
    (
        bar_ref, new_ref, avail_ref, high_ref, low_ref, invest_ref, square_ref, load_ref,
        flow_ref, angbar_ref, pownew_ref, powbar_ref,
    ) = refs[-12:]
    others = refs[:-12]
    rows, _, buses = gen_ref.shape
    unroll = divisor(rows, 7)
    region = lax.axis_index("region")
    pieces = 2 if swap else 1
    width = BUS // pieces
    blocks = buses // BLOCK
    shift = region * blocks if swap else 0
    for i in range(blocks):
        for j in range(BUS // BLOCK):
            at = (slice(i * BLOCK, (i + 1) * BLOCK), slice(j * BLOCK, (j + 1) * BLOCK))
            place = lax.rem(j + shift, BUS // BLOCK)
            coupled = pat_s[region * blocks + i, place].astype(F32)
            source = net_ref[at[0], pl.ds(pl.multiple_of(place * BLOCK, BLOCK), BLOCK)]
            high, low = split(source * coupled)
            high_ref[at] = high
            low_ref[at] = low

    mask = mask_ref[...].astype(F32)
    cost = vc_ref[...]
    live = live_s[0] - lax.axis_index("hour") * rows

    def step(t, carry, first=False):
        before, limit_sum, ramp_sum, squares = carry
        gen, lim, ramp = gen_ref[t], lim_ref[t], ramp_ref[t]
        alive = jnp.where(t < live, 1.0, 0.0).astype(F32)
        avail = av_ref[t].astype(F32) * mask * alive
        avail_ref[t] = avail
        limit_sum += avail * lim
        ramp_sum += ramp
        if not first:
            dual = jnp.broadcast_to(bal_ref[pl.ds(t, 1), :], (TECH, buses))
            new = jnp.maximum(0.0, gen - primal_step * (cost + dual + lim + before - ramp))
            squares += (new - gen) ** 2
            new_ref[t] = new
            bar_ref[t] = 2.0 * new - gen
        else:
            bar_ref[t] = gen
        return ramp, limit_sum, ramp_sum, squares

    carry = (jnp.zeros((TECH, buses), F32),) * 4
    for t in range(unroll):
        carry = step(t, carry, t == 0)

    def several(j, carry):
        for k in range(unroll):
            carry = step(j * unroll + k, carry)
        return carry

    _, limit_sum, ramp_sum, squares = lax.fori_loop(1, rows // unroll, several, carry)
    invest_ref[...] = limit_sum + rr_ref[...] * ramp_sum
    flow = network_product(others, high_ref, low_ref)
    flow_ref[...] = flow
    ang_step = primal_step * flow
    angbar_ref[...] = ang_ref[...] + 2.0 * ang_step
    pow_old = pow_ref[...]
    pow_new = pow_old - primal_step * (bal_ref[...] + sto_ref[...])
    pownew_ref[...] = pow_new
    powbar_ref[...] = 2.0 * pow_new - pow_old
    square_ref[...] = add_squares(squares, ang_step, pow_new - pow_old)
    row = lax.broadcasted_iota(jnp.int32, (rows, buses), 0)
    load_ref[...] = jnp.where(row < live, demand_ref[...], 0.0)


def fold_rows(square):
    rows = square.shape[0]
    full = rows // TECH * TECH
    total = jnp.sum(square[:full].reshape(full // TECH, TECH, square.shape[1]), axis=0)
    return total, square[full:]


def layout(buses, lone):
    width = max(BLOCK, buses * (1 << (lone + 1).bit_length() - 1) // TECH)
    return width, buses // width


def put_totals(out_ref, lone, invest, squares, rows_of_one):
    buses = invest.shape[1]
    width, parts = layout(buses, lone)
    lanes = slice(buses, buses + width)
    out_ref[:, :buses] = invest
    out_ref[:, lanes] = jnp.zeros((TECH, width), F32)
    for i, row in enumerate((jnp.sum(squares, axis=0, keepdims=True), *rows_of_one)):
        for j in range(parts):
            out_ref[i * parts + j : i * parts + j + 1, lanes] = row[:, j * width : (j + 1) * width]


def put_cubes(out_ref, lone, *cubes):
    start = cubes[0].shape[1] + layout(cubes[0].shape[1], lone)[0]
    for i, cube in enumerate(cubes):
        out_ref[:, start + i * cube.shape[1] : start + (i + 1) * cube.shape[1]] = cube


def get_totals(entries, buses, lone, here_ref, squares_ref, other_ref):
    width, parts = layout(buses, lone)
    at = (slice(0, parts), slice(buses, buses + width))
    squares = jnp.sum(squares_ref[at] + other_ref[at])
    return here_ref[:, :buses], dual_scale * lax.rsqrt(jnp.full((1, 1), squares / entries + 1e-06, F32))


def get_row(buses, lone, index, read):
    width, parts = layout(buses, lone)
    lanes = slice(buses, buses + width)
    return jnp.concatenate(
        [read((slice(i, i + 1), lanes)) for i in range(index * parts, (index + 1) * parts)], axis=1
    )


def get_cube(buses, lone, index, read):
    start = buses + layout(buses, lone)[0] + index * buses
    return read((slice(None), slice(start, start + buses)))


def neighbour(passed, ahead, index):
    device = lax.axis_index("hour")
    block = passed[0][index]
    for k in range(1, len(passed)):
        low = lax.rem(device, 1 << k)
        differs = low == (1 << k) - 1 if ahead else low == 0
        block = jnp.where(differs, passed[k][index], block)
    return block


def add_squares(total, *terms):
    for term in terms:
        full, rest = fold_rows(term * term)
        total = total + full
        if rest.shape[0]:
            rest = jnp.sum(rest, axis=0, keepdims=True)
            row = lax.broadcasted_iota(jnp.int32, total.shape, 0)
            total = total + jnp.where(row == 0, rest, 0.0)
    return total


def first_body(
    bar_ref, lim_ref, ramp_ref, halo_ref, vc_ref, invest_ref, square_ref, bal_ref, lev_ref, sto_ref, powbar_ref,
    row_ref, levnew_ref, levbar_ref, total_ref, shift_ref,
):
    rows, _, buses = bar_ref.shape
    gen = bar_ref[0]
    dual = jnp.broadcast_to(bal_ref[0:1, :], (TECH, buses))
    new = jnp.maximum(
        0.0, gen - primal_step * (vc_ref[...] + dual + lim_ref[0] + halo_ref[:TECH] - ramp_ref[0])
    )
    row_ref[...] = new
    sto = sto_ref[...]
    shift_ref[8 : 8 + rows] = sto
    shift_ref[7:8] = halo_ref[TECH : TECH + 1]
    lev_old = lev_ref[...]
    lev_new = jnp.maximum(0.0, lev_old - primal_step * (shift_ref[7 : 7 + rows] - sto))
    levnew_ref[...] = lev_new
    levbar_ref[...] = 2.0 * lev_new - lev_old
    put_totals(
        total_ref, 3, invest_ref[...], add_squares(square_ref[...], new - gen, lev_new - lev_old),
        (levbar_ref[0:1], levbar_ref[rows - 1 : rows], powbar_ref[rows - 1 : rows]),
    )
    odd = lax.rem(lax.axis_index("hour"), 2) == 1
    begin, end = 2.0 * new - gen, bar_ref[rows - 1]
    put_cubes(total_ref, 3, jnp.where(odd, end, begin), jnp.where(odd, begin, end))


def residual_one_body(
    pieces, bar_ref, row_ref, powbar_ref, load_ref, high_ref, low_ref, *refs,
):
    sources, (out_ref, sum_ref) = refs[:pieces], refs[pieces:]
    rows, _, buses = bar_ref.shape
    unroll = divisor(rows, 7)
    flow = network_product(sources, high_ref, low_ref)

    def several(j, _):
        for k in range(unroll):
            t = j * unroll + k
            sum_ref[pl.ds(t, 1), :] = jnp.sum(bar_ref[t], axis=0, keepdims=True)
        return 0

    lax.fori_loop(0, rows // unroll, several, 0)
    sum_ref[0:1] = jnp.sum(2.0 * row_ref[...] - bar_ref[0], axis=0, keepdims=True)
    out_ref[...] = sum_ref[...] + powbar_ref[...] - flow - load_ref[...]


def product_body(pieces, high_ref, low_ref, *refs):
    refs[pieces][...] = network_product(refs[:pieces], high_ref, low_ref)


def capacity_of(hours, cap_ref, inv_ref, invest):
    return jnp.maximum(0.0, cap_ref[...] - capacity_step * (inv_ref[...] - invest / float(hours)))


def middle_body(
    hours, entries, steps, here_ref, squares_ref, other_ref, *refs,
):
    passed, refs = refs[:steps], refs[steps:]
    (
        cap_ref, inv_ref, rr_ref, vc_ref,
        bar_ref, new_ref, row_ref, lim_ref, ramp_ref, avail_ref, halo_ref,
        bal_ref, res_ref, resflow_ref, flow_ref, ang_ref, pownew_ref, powbar_ref, levnew_ref, levbar_ref, sto_ref,
        capout_ref, gen2_ref, lim2_ref, ramp2_ref, bal2_ref, sto2_ref, ang2_ref, angbar2_ref, pow2_ref,
        powbar2_ref, lev2_ref, levbar2_ref, out_ref, shift_ref,
    ) = refs
    rows, _, buses = bar_ref.shape
    invest, step_size = get_totals(entries, buses, 3, here_ref, squares_ref, other_ref)
    from_next = functools.partial(neighbour, passed, True)
    from_last = functools.partial(neighbour, passed, False)
    lev_front = get_row(buses, 3, 1, from_next)
    lev_behind = get_row(buses, 3, 2, from_last)
    pow_behind = get_row(buses, 3, 3, from_last)
    odd = lax.rem(lax.axis_index("hour"), 2) == 1
    direct = get_cube(buses, 3, 1, passed[0].__getitem__)
    bar_front = jnp.where(odd, get_cube(buses, 3, 0, from_next), direct)
    bar_behind = jnp.where(odd, direct, get_cube(buses, 3, 0, from_last))
    cap_new = capacity_of(hours, cap_ref, inv_ref, invest)
    capout_ref[...] = cap_new
    cap_bar = 2.0 * cap_new - cap_ref[...]
    rate = rr_ref[...]
    ramp_cap = rate * cap_bar
    cost = vc_ref[...]

    bal = bal_ref[...] + step_size * res_ref[...]
    bal2_ref[...] = bal
    lev_bar, pow_bar = levbar_ref[...], powbar_ref[...]
    shift_ref[8 : 8 + rows] = lev_bar
    shift_ref[8 + rows : 9 + rows] = lev_front
    sto = sto_ref[...] + step_size * (shift_ref[9 : 9 + rows] - lev_bar + pow_bar)
    sto2_ref[...] = sto
    sto_before = halo_ref[TECH : TECH + 1] + step_size * (
        levbar_ref[0:1] - lev_behind + pow_behind
    )
    shift_ref[8 : 8 + rows] = sto
    shift_ref[7:8] = sto_before
    ang_step = primal_step * (flow_ref[...] + step_size * resflow_ref[...])
    ang_old = ang_ref[...] + primal_step * flow_ref[...]
    ang2_ref[...] = ang_old + ang_step
    angbar2_ref[...] = ang_old + 2.0 * ang_step
    pow_old = pownew_ref[...]
    pow_new = pow_old - primal_step * (bal + sto)
    pow2_ref[...] = pow_new
    powbar2_ref[...] = 2.0 * pow_new - pow_old
    lev_old = levnew_ref[...]
    lev_new = jnp.maximum(0.0, lev_old - primal_step * (shift_ref[7 : 7 + rows] - sto))
    lev2_ref[...] = lev_new
    levbar2_ref[...] = 2.0 * lev_new - lev_old
    squares = add_squares(
        jnp.zeros((TECH, buses), F32), ang_step, pow_new - pow_old, lev_new - lev_old
    )

    unroll = divisor(rows, 7)

    def step(t, carry, first=False, last=False):
        bar, before, limit_sum, ramp_sum, squares = carry
        old = row_ref[...] if first else new_ref[t]
        bar_next = bar_front if last else bar_ref[t + 1]
        avail = avail_ref[t]
        lim = jnp.maximum(0.0, lim_ref[t] + step_size * (bar - avail * cap_bar))
        ramp = jnp.maximum(0.0, ramp_ref[t] + step_size * (bar_next - bar - ramp_cap))
        dual = jnp.broadcast_to(bal2_ref[pl.ds(t, 1), :], (TECH, buses))
        gen = jnp.maximum(0.0, old - primal_step * (cost + dual + lim + before - ramp))
        squares += (gen - old) ** 2
        limit_sum += avail * lim
        ramp_sum += ramp
        gen2_ref[t] = gen
        lim2_ref[t] = lim
        ramp2_ref[t] = ramp
        if first:
            put_cubes(out_ref, 1, 2.0 * gen - old)
        return bar_next, ramp, limit_sum, ramp_sum, squares

    bar = 2.0 * row_ref[...] - bar_ref[0]
    before = jnp.maximum(0.0, halo_ref[:TECH] + step_size * (bar - bar_behind - ramp_cap))
    zero = jnp.zeros((TECH, buses), F32)
    carry = (bar, before, zero, zero, squares)
    for t in range(unroll):
        carry = step(t, carry, first=t == 0)

    def several(j, carry):
        for k in range(unroll):
            carry = step(j * unroll + k, carry)
        return carry

    carry = lax.fori_loop(1, rows // unroll - 1, several, carry)
    for t in range(rows - unroll, rows):
        carry = step(t, carry, last=t == rows - 1)
    _, _, limit_sum, ramp_sum, squares = carry
    put_totals(out_ref, 1, limit_sum + rate * ramp_sum, squares, (levbar2_ref[0:1],))


def residual_two_body(
    pieces, gen_ref, ang_ref, lev_ref, pow_ref, new_ref, row_ref, powbar_ref, load_ref, high_ref, low_ref, *refs,
):
    sources, refs = refs[:pieces], refs[pieces:]
    out_ref, bar_ref, gen_h, ang_h, lev_h, pow_h, sum_ref, sems = refs
    copies = [
        pltpu.make_async_copy(source, target, sems.at[k])
        for k, (source, target) in enumerate(
            ((gen_ref, gen_h), (ang_ref, ang_h), (lev_ref, lev_h), (pow_ref, pow_h))
        )
    ]
    for copy in copies:
        copy.start()
    rows, _, buses = gen_ref.shape
    unroll = divisor(rows, 7)
    flow = network_product(sources, high_ref, low_ref)

    def one(t, old):
        bar = 2.0 * gen_ref[t] - old
        bar_ref[t] = bar
        sum_ref[pl.ds(t, 1), :] = jnp.sum(bar, axis=0, keepdims=True)

    for t in range(unroll):
        one(t, new_ref[t] if t else row_ref[...])

    def several(j, _):
        for k in range(unroll):
            one(j * unroll + k, new_ref[j * unroll + k])
        return 0

    lax.fori_loop(1, rows // unroll, several, 0)
    out_ref[...] = sum_ref[...] + powbar_ref[...] - flow - load_ref[...]
    for copy in copies:
        copy.wait()


def last_body(
    hours, entries, steps, here_ref, squares_ref, other_ref, *refs,
):
    passed, refs = refs[:steps], refs[steps:]
    (
        cap_ref, inv_ref, rr_ref,
        bar_ref, lim_ref, ramp_ref, avail_ref, bal_ref, res_ref, sto_ref, levbar_ref, powbar_ref,
        cap_h, lim_h, ramp_h, bal_h, sto_h, cap_v, lim_v, ramp_v, bal_v, sto_v, shift_ref, sems, small_sems,
    ) = refs
    rows, _, buses = bar_ref.shape
    chunk = divisor(rows, 28)
    unroll = divisor(chunk, 7)
    chunks = rows // chunk
    invest, step_size = get_totals(entries, buses, 1, here_ref, squares_ref, other_ref)
    from_next = functools.partial(neighbour, passed, True)
    lev_front = get_row(buses, 1, 1, from_next)
    bar_front = get_cube(buses, 1, 0, from_next)
    cap_new = capacity_of(hours, cap_ref, inv_ref, invest)
    cap_v[...] = cap_new
    bal_v[...] = bal_ref[...] + step_size * res_ref[...]
    lev_bar = levbar_ref[...]
    shift_ref[8 : 8 + rows] = lev_bar
    shift_ref[8 + rows : 9 + rows] = lev_front
    sto_v[...] = sto_ref[...] + step_size * (shift_ref[9 : 9 + rows] - lev_bar + powbar_ref[...])
    small = [
        pltpu.make_async_copy(source, target, small_sems.at[k])
        for k, (source, target) in enumerate(((cap_v, cap_h), (bal_v, bal_h), (sto_v, sto_h)))
    ]
    for copy in small:
        copy.start()
    cap_bar = 2.0 * cap_new - cap_ref[...]
    ramp_cap = rr_ref[...] * cap_bar

    def copies(i):
        rows_here = pl.ds(i * chunk, chunk)
        return [
            pltpu.make_async_copy(source.at[rows_here], target.at[rows_here], sems.at[i, k])
            for k, (source, target) in enumerate(((lim_v, lim_h), (ramp_v, ramp_h)))
        ]

    def step(t, bar, last=False):
        bar_next = bar_front if last else bar_ref[t + 1]
        lim_v[t] = jnp.maximum(0.0, lim_ref[t] + step_size * (bar - avail_ref[t] * cap_bar))
        ramp_v[t] = jnp.maximum(0.0, ramp_ref[t] + step_size * (bar_next - bar - ramp_cap))
        return bar_next

    bar = bar_ref[0]
    for i in range(chunks):
        end = (i + 1) * chunk
        stop = end - unroll if i == chunks - 1 else end

        def several(j, bar, start=i * chunk):
            for k in range(unroll):
                bar = step(start + j * unroll + k, bar)
            return bar

        bar = lax.fori_loop(0, (stop - i * chunk) // unroll, several, bar)
        for t in range(stop, end):
            bar = step(t, bar, last=t == rows - 1)
        for copy in copies(i):
            copy.start()
    for i in range(chunks):
        for copy in copies(i):
            copy.wait()
    for copy in small:
        copy.wait()


def per_device(
    demand,
    avail_factor,
    tech_mask,
    var_cost,
    inv_cost,
    ramp_rate,
    network,
    pattern,
    live_hours,
    generation,
    angles,
    levels,
    net_power,
    capacity,
    balance_dual,
    storage_dual,
    limit_dual,
    ramp_dual,
):
    rows, buses = demand.shape
    hours = rows * lax.axis_size("hour")
    entries = float(hours * (TECH + 3) * BUS)
    swap = lax.axis_size("region") == 2
    pieces = 2 if swap else 1
    cube, flat, tech = (rows, TECH, buses), (rows, buses), (TECH, buses)
    shift = pltpu.VMEM((rows + 24, buses), F32)
    chunks = rows // divisor(rows, 28)

    def all_buses(block):
        if swap:
            return block, partner(block, "region", 1)
        return (lax.all_gather(block, "region", axis=1, tiled=True),)

    steps = len(distances("hour"))

    def totals(block, lone, once, *work):
        row = lax.broadcasted_iota(jnp.int32, block.shape, 0)
        lane = lax.broadcasted_iota(jnp.int32, block.shape, 1)
        width, parts = layout(buses, lone)
        adds = (lane < buses) | ((lane < buses + width) & (row < parts))
        passed = []
        for k, distance in enumerate(distances("hour")):
            got = partner(block, "hour", distance)
            passed.append(got)
            if k < len(work) and work[k]:
                block = after(block, work[k]())
            block = got + jnp.where(adds[:, : block.shape[1]], block, 0.0)
            if k == 0:
                block = block[:, : block.shape[1] - once]
        squares = block
        *inner, outer = distances("region")
        for distance in inner:
            squares = squares + partner(squares, "region", distance)
        return block, squares, partner(squares, "region", outer), passed

    (halo,) = call(
        pack_body,
        (ramp_dual, storage_dual, generation, limit_dual, network, avail_factor, demand, tech_mask,
         angles, net_power, levels),
        [HBM] * 11,
        [((2 * TECH, buses), F32)],
        scratch=(pltpu.VMEM((rows - (rows - 1) // TECH * TECH, buses), F32), pltpu.SemaphoreType.DMA((2,))),
        moved=1 << 28,
        name="pack",
    )
    balances = all_buses(balance_dual)
    halo = shifted(halo, "hour", 1)

    bar, new, avail, high, low, invest, square, load, flow, ang_bar, pow_new, pow_bar = call(
        functools.partial(load_body, swap),
        (generation, limit_dual, ramp_dual, avail_factor, network, tech_mask, var_cost, ramp_rate,
         balance_dual, demand, pattern, live_hours, angles, net_power, storage_dual, *balances),
        [VMEM] * 10 + [SMEM] * 2 + [VMEM] * (3 + pieces),
        [(cube, F32)] * 3 + [((buses, BUS), jnp.bfloat16)] * 2 + [(tech, F32)] * 2 + [(flat, F32)] * 5,
        name="load",
    )
    lim, ramp = limit_dual, ramp_dual
    row, lev_new, lev_bar, total = call(
        first_body,
        (bar, lim, ramp, halo, var_cost, invest, square, balance_dual, levels, storage_dual, pow_bar),
        [VMEM] * 11,
        [(tech, F32)] + [(flat, F32)] * 2 + [((TECH, 3 * buses + layout(buses, 3)[0]), F32)],
        scratch=(shift,),
        name="first",
    )
    sources = all_buses(ang_bar)
    made = {}

    def residual():
        (made["res"],) = call(
            functools.partial(residual_one_body, pieces),
            (bar, row, pow_bar, load, high, low, *sources),
            [VMEM] * (6 + pieces),
            [(flat, F32)],
            scratch=(pltpu.VMEM(flat, F32),),
            name="residual1",
        )
        return made["res"]

    def product():
        (made["flow"],) = call(
            functools.partial(product_body, pieces),
            (high, low, *all_buses(made["res"])),
            [VMEM] * (2 + pieces),
            [(flat, F32)],
            name="product",
        )
        return made["flow"]

    here, squares, other, passed = totals(total, 3, buses, None, residual, None, product)
    res, res_flow = made["res"], made["flow"]
    (
        cap, gen2, lim1, ramp1, bal1, sto1, ang2, ang_bar2, pow2, pow_bar2, lev2, lev_bar2, total2,
    ) = call(
        functools.partial(middle_body, hours, entries, steps),
        (here, squares, other, *passed, capacity, inv_cost, ramp_rate, var_cost, bar, new, row, lim, ramp, avail,
         halo, balance_dual, res, res_flow, flow, angles, pow_new, pow_bar, lev_new, lev_bar,
         storage_dual),
        [VMEM] * (24 + steps),
        [(tech, F32)] + [(cube, F32)] * 3 + [(flat, F32)] * 8 + [((TECH, 2 * buses + layout(buses, 1)[0]), F32)],
        scratch=(shift,),
        name="middle",
    )
    sources2 = all_buses(ang_bar2)

    def residual2():
        made["two"] = call(
            functools.partial(residual_two_body, pieces),
            (gen2, ang2, lev2, pow2, new, row, pow_bar2, load, high, low, *sources2),
            [VMEM] * (10 + pieces),
            [(flat, F32), (cube, F32), (cube, F32)] + [(flat, F32)] * 3,
            out_specs=[VMEM] * 2 + [HBM] * 4,
            scratch=(pltpu.VMEM(flat, F32), pltpu.SemaphoreType.DMA((4,))),
            name="residual2",
        )
        return made["two"][0]

    here2, squares2, other2, passed2 = totals(total2, 1, 0, None, residual2)
    res2, bar2, gen2, ang2, lev2, pow2 = made["two"]
    cap2, lim2, ramp2, bal2, sto2 = call(
        functools.partial(last_body, hours, entries, steps),
        (here2, squares2, other2, *passed2, cap, inv_cost, ramp_rate, bar2, lim1, ramp1, avail, bal1, res2, sto1,
         lev_bar2, pow_bar2),
        [VMEM] * (15 + steps),
        [(tech, F32), (cube, F32), (cube, F32), (flat, F32), (flat, F32)],
        out_specs=[HBM] * 5,
        scratch=(
            pltpu.VMEM(tech, F32), pltpu.VMEM(cube, F32), pltpu.VMEM(cube, F32), pltpu.VMEM(flat, F32),
            pltpu.VMEM(flat, F32), shift, pltpu.SemaphoreType.DMA((chunks, 2)), pltpu.SemaphoreType.DMA((3,)),
        ),
        name="last",
    )
    return gen2, ang2, lev2, pow2, cap2, bal2, sto2, lim2, ramp2


def solution(mesh):
    return jax.shard_map(
        per_device,
        mesh=mesh,
        in_specs=(
            P("hour", "region"),
            P("hour", None, "region"),
            P(None, "region"),
            P(None, "region"),
            P(None, "region"),
            P(None, "region"),
            P("region", None),
            P(),
            P(),
            P("hour", None, "region"),
            P("hour", "region"),
            P("hour", "region"),
            P("hour", "region"),
            P(None, "region"),
            P("hour", "region"),
            P("hour", "region"),
            P("hour", None, "region"),
            P("hour", None, "region"),
        ),
        out_specs=(
            P("hour", None, "region"),
            P("hour", "region"),
            P("hour", "region"),
            P("hour", "region"),
            P(None, "region"),
            P("hour", "region"),
            P("hour", "region"),
            P("hour", None, "region"),
            P("hour", None, "region"),
        ),
        check_vma=False,
    )
```

```python
import functools

import jax
import jax.numpy as jnp
from jax import lax
from jax.experimental import pallas as pl
from jax.experimental.pallas import tpu as pltpu
from jax.sharding import PartitionSpec as P

BUS = 1024
TECH = 8
BLOCK = 128
ITERS = 2

primal_step = 0.2
capacity_step = 4.0
dual_scale = 0.06

F32 = jnp.float32
VMEM = pl.BlockSpec(memory_space=pltpu.VMEM)
SMEM = pl.BlockSpec(memory_space=pltpu.SMEM)
HBM = pl.BlockSpec(memory_space=pltpu.HBM)


def shifted(block, axis, distance):
    devices = range(lax.axis_size(axis))
    route = [((i - distance) % len(devices), i) for i in devices]
    return lax.ppermute(block, axis, route)


def partner(block, axis, distance):
    return lax.ppermute(block, axis, [(i, i ^ distance) for i in range(lax.axis_size(axis))])


def distances(axis):
    size = lax.axis_size(axis)
    return [1 << i for i in range(size.bit_length() - 1)]


def summed(block, axis):
    for distance in distances(axis):
        block = block + partner(block, axis, distance)
    return block


def after(block, earlier):
    return lax.optimization_barrier((block, earlier))[0]


def divisor(extent, most):
    return max(d for d in range(1, most + 1) if extent % d == 0)


def split(value):
    high = value.astype(jnp.bfloat16)
    return high, (value - high.astype(F32)).astype(jnp.bfloat16)


def network_product(sources, high_ref, low_ref):
    total, at = None, 0
    for source in sources:
        columns = slice(at, at + source.shape[1])
        at += source.shape[1]
        high, low = split(source[...])
        for left, right in ((high, high_ref), (low, high_ref), (high, low_ref)):
            term = lax.dot_general(
                left, right[:, columns], (((1,), (1,)), ((), ())), preferred_element_type=F32
            )
            total = term if total is None else total + term
    return total


def call(body, operands, specs, outs, out_specs=None, scratch=(), flops=1 << 22, moved=1 << 23, room=8, name=None):
    operands = [
        pltpu.with_memory_space_constraint(operand, pltpu.HBM) if spec is HBM else operand
        for operand, spec in zip(operands, specs)
    ]
    return pl.pallas_call(
        body,
        out_shape=[jax.ShapeDtypeStruct(shape, dtype) for shape, dtype in outs],
        in_specs=specs,
        out_specs=out_specs or [VMEM] * len(outs),
        scratch_shapes=list(scratch),
        compiler_params=pltpu.CompilerParams(vmem_limit_bytes=room << 20),
        cost_estimate=pl.CostEstimate(flops=flops, bytes_accessed=moved, transcendentals=0),
        name=name,
    )(*operands)


def pack_body(ramp_h, sto_h, *refs):
    halo_ref, sto_v, sems = refs[-3:]
    rows = ramp_h.shape[0]
    start = (rows - 1) // TECH * TECH
    copies = [
        pltpu.make_async_copy(ramp_h.at[rows - 1], halo_ref.at[pl.ds(0, TECH)], sems.at[0]),
        pltpu.make_async_copy(sto_h.at[pl.ds(start, rows - start)], sto_v, sems.at[1]),
    ]
    for copy in copies:
        copy.start()
    for copy in copies:
        copy.wait()
    halo_ref[TECH:] = jnp.broadcast_to(sto_v[rows - 1 - start : rows - start], (TECH, sto_v.shape[1]))


def load_body(
    swap, gen_ref, lim_ref, ramp_ref, av_ref, net_ref, mask_ref, vc_ref, rr_ref, bal_ref, demand_ref, pat_s, live_s,
    ang_ref, pow_ref, sto_ref, *refs,
):
    (
        bar_ref, new_ref, avail_ref, high_ref, low_ref, invest_ref, square_ref, load_ref,
        flow_ref, angbar_ref, pownew_ref, powbar_ref,
    ) = refs[-12:]
    others = refs[:-12]
    rows, _, buses = gen_ref.shape
    unroll = divisor(rows, 7)
    region = lax.axis_index("region")
    pieces = 2 if swap else 1
    width = BUS // pieces
    blocks = buses // BLOCK
    shift = region * blocks if swap else 0
    for i in range(blocks):
        for j in range(BUS // BLOCK):
            at = (slice(i * BLOCK, (i + 1) * BLOCK), slice(j * BLOCK, (j + 1) * BLOCK))
            place = lax.rem(j + shift, BUS // BLOCK)
            coupled = pat_s[region * blocks + i, place].astype(F32)
            source = net_ref[at[0], pl.ds(pl.multiple_of(place * BLOCK, BLOCK), BLOCK)]
            high, low = split(source * coupled)
            high_ref[at] = high
            low_ref[at] = low

    mask = mask_ref[...].astype(F32)
    cost = vc_ref[...]
    live = live_s[0] - lax.axis_index("hour") * rows

    def step(t, carry, first=False):
        before, limit_sum, ramp_sum, squares = carry
        gen, lim, ramp = gen_ref[t], lim_ref[t], ramp_ref[t]
        alive = jnp.where(t < live, 1.0, 0.0).astype(F32)
        avail = av_ref[t].astype(F32) * mask * alive
        avail_ref[t] = avail
        limit_sum += avail * lim
        ramp_sum += ramp
        if not first:
            dual = jnp.broadcast_to(bal_ref[pl.ds(t, 1), :], (TECH, buses))
            new = jnp.maximum(0.0, gen - primal_step * (cost + dual + lim + before - ramp))
            squares += (new - gen) ** 2
            new_ref[t] = new
            bar_ref[t] = 2.0 * new - gen
        else:
            bar_ref[t] = gen
        return ramp, limit_sum, ramp_sum, squares

    carry = (jnp.zeros((TECH, buses), F32),) * 4
    for t in range(unroll):
        carry = step(t, carry, t == 0)

    def several(j, carry):
        for k in range(unroll):
            carry = step(j * unroll + k, carry)
        return carry

    _, limit_sum, ramp_sum, squares = lax.fori_loop(1, rows // unroll, several, carry)
    invest_ref[...] = limit_sum + rr_ref[...] * ramp_sum
    flow = network_product(others, high_ref, low_ref)
    flow_ref[...] = flow
    ang_step = primal_step * flow
    angbar_ref[...] = ang_ref[...] + 2.0 * ang_step
    pow_old = pow_ref[...]
    pow_new = pow_old - primal_step * (bal_ref[...] + sto_ref[...])
    pownew_ref[...] = pow_new
    powbar_ref[...] = 2.0 * pow_new - pow_old
    square_ref[...] = add_squares(squares, ang_step, pow_new - pow_old)
    row = lax.broadcasted_iota(jnp.int32, (rows, buses), 0)
    load_ref[...] = jnp.where(row < live, demand_ref[...], 0.0)


def fold_rows(square):
    rows = square.shape[0]
    full = rows // TECH * TECH
    total = jnp.sum(square[:full].reshape(full // TECH, TECH, square.shape[1]), axis=0)
    return total, square[full:]


def layout(buses, lone):
    width = max(BLOCK, buses * (1 << (lone + 1).bit_length() - 1) // TECH)
    return width, buses // width


def put_totals(out_ref, lone, invest, squares, rows_of_one):
    buses = invest.shape[1]
    width, parts = layout(buses, lone)
    lanes = slice(buses, buses + width)
    out_ref[:, :buses] = invest
    out_ref[:, lanes] = jnp.zeros((TECH, width), F32)
    for i, row in enumerate((jnp.sum(squares, axis=0, keepdims=True), *rows_of_one)):
        for j in range(parts):
            out_ref[i * parts + j : i * parts + j + 1, lanes] = row[:, j * width : (j + 1) * width]


def put_cubes(out_ref, lone, *cubes):
    start = cubes[0].shape[1] + layout(cubes[0].shape[1], lone)[0]
    for i, cube in enumerate(cubes):
        out_ref[:, start + i * cube.shape[1] : start + (i + 1) * cube.shape[1]] = cube


def get_totals(entries, buses, lone, here_ref, squares_ref, other_ref):
    width, parts = layout(buses, lone)
    at = (slice(0, parts), slice(buses, buses + width))
    squares = jnp.sum(squares_ref[at] + other_ref[at])
    return here_ref[:, :buses], dual_scale * lax.rsqrt(jnp.full((1, 1), squares / entries + 1e-06, F32))


def get_row(buses, lone, index, read):
    width, parts = layout(buses, lone)
    lanes = slice(buses, buses + width)
    return jnp.concatenate(
        [read((slice(i, i + 1), lanes)) for i in range(index * parts, (index + 1) * parts)], axis=1
    )


def get_cube(buses, lone, index, read):
    start = buses + layout(buses, lone)[0] + index * buses
    return read((slice(None), slice(start, start + buses)))


def neighbour(passed, ahead, index):
    device = lax.axis_index("hour")
    block = passed[0][index]
    for k in range(1, len(passed)):
        low = lax.rem(device, 1 << k)
        differs = low == (1 << k) - 1 if ahead else low == 0
        block = jnp.where(differs, passed[k][index], block)
    return block


def add_squares(total, *terms):
    for term in terms:
        full, rest = fold_rows(term * term)
        total = total + full
        if rest.shape[0]:
            rest = jnp.sum(rest, axis=0, keepdims=True)
            row = lax.broadcasted_iota(jnp.int32, total.shape, 0)
            total = total + jnp.where(row == 0, rest, 0.0)
    return total


def first_body(
    bar_ref, lim_ref, ramp_ref, halo_ref, vc_ref, invest_ref, square_ref, bal_ref, lev_ref, sto_ref, powbar_ref,
    row_ref, levnew_ref, levbar_ref, total_ref, shift_ref,
):
    rows, _, buses = bar_ref.shape
    gen = bar_ref[0]
    dual = jnp.broadcast_to(bal_ref[0:1, :], (TECH, buses))
    new = jnp.maximum(
        0.0, gen - primal_step * (vc_ref[...] + dual + lim_ref[0] + halo_ref[:TECH] - ramp_ref[0])
    )
    row_ref[...] = new
    sto = sto_ref[...]
    shift_ref[8 : 8 + rows] = sto
    shift_ref[7:8] = halo_ref[TECH : TECH + 1]
    lev_old = lev_ref[...]
    lev_new = jnp.maximum(0.0, lev_old - primal_step * (shift_ref[7 : 7 + rows] - sto))
    levnew_ref[...] = lev_new
    levbar_ref[...] = 2.0 * lev_new - lev_old
    put_totals(
        total_ref, 3, invest_ref[...], add_squares(square_ref[...], new - gen, lev_new - lev_old),
        (levbar_ref[0:1], levbar_ref[rows - 1 : rows], powbar_ref[rows - 1 : rows]),
    )
    odd = lax.rem(lax.axis_index("hour"), 2) == 1
    begin, end = 2.0 * new - gen, bar_ref[rows - 1]
    put_cubes(total_ref, 3, jnp.where(odd, end, begin), jnp.where(odd, begin, end))


def residual_one_body(
    pieces, bar_ref, row_ref, powbar_ref, load_ref, high_ref, low_ref, *refs,
):
    sources, (out_ref, sum_ref) = refs[:pieces], refs[pieces:]
    rows, _, buses = bar_ref.shape
    unroll = divisor(rows, 7)
    flow = network_product(sources, high_ref, low_ref)

    def several(j, _):
        for k in range(unroll):
            t = j * unroll + k
            sum_ref[pl.ds(t, 1), :] = jnp.sum(bar_ref[t], axis=0, keepdims=True)
        return 0

    lax.fori_loop(0, rows // unroll, several, 0)
    sum_ref[0:1] = jnp.sum(2.0 * row_ref[...] - bar_ref[0], axis=0, keepdims=True)
    out_ref[...] = sum_ref[...] + powbar_ref[...] - flow - load_ref[...]


def product_body(pieces, high_ref, low_ref, *refs):
    refs[pieces][...] = network_product(refs[:pieces], high_ref, low_ref)


def capacity_of(hours, cap_ref, inv_ref, invest):
    return jnp.maximum(0.0, cap_ref[...] - capacity_step * (inv_ref[...] - invest / float(hours)))


def middle_body(
    hours, entries, steps, here_ref, squares_ref, other_ref, *refs,
):
    passed, refs = refs[:steps], refs[steps:]
    (
        cap_ref, inv_ref, rr_ref, vc_ref,
        bar_ref, new_ref, row_ref, lim_ref, ramp_ref, avail_ref, halo_ref,
        bal_ref, res_ref, resflow_ref, flow_ref, ang_ref, pownew_ref, powbar_ref, levnew_ref, levbar_ref, sto_ref,
        capout_ref, gen2_ref, lim2_ref, ramp2_ref, bal2_ref, sto2_ref, ang2_ref, angbar2_ref, pow2_ref,
        powbar2_ref, lev2_ref, levbar2_ref, out_ref, shift_ref, cut_ref,
    ) = refs
    rows, _, buses = bar_ref.shape
    invest, step_size = get_totals(entries, buses, 3, here_ref, squares_ref, other_ref)
    from_next = functools.partial(neighbour, passed, True)
    from_last = functools.partial(neighbour, passed, False)
    lev_front = get_row(buses, 3, 1, from_next)
    lev_behind = get_row(buses, 3, 2, from_last)
    pow_behind = get_row(buses, 3, 3, from_last)
    odd = lax.rem(lax.axis_index("hour"), 2) == 1
    direct = get_cube(buses, 3, 1, passed[0].__getitem__)
    bar_front = jnp.where(odd, get_cube(buses, 3, 0, from_next), direct)
    bar_behind = jnp.where(odd, direct, get_cube(buses, 3, 0, from_last))
    cap_new = capacity_of(hours, cap_ref, inv_ref, invest)
    capout_ref[...] = cap_new
    cap_bar = 2.0 * cap_new - cap_ref[...]
    rate = rr_ref[...]
    ramp_cap = rate * cap_bar
    cost = vc_ref[...]

    bal = bal_ref[...] + step_size * res_ref[...]
    bal2_ref[...] = bal
    lev_bar, pow_bar = levbar_ref[...], powbar_ref[...]
    shift_ref[8 : 8 + rows] = lev_bar
    shift_ref[8 + rows : 9 + rows] = lev_front
    sto = sto_ref[...] + step_size * (shift_ref[9 : 9 + rows] - lev_bar + pow_bar)
    sto2_ref[...] = sto
    sto_before = halo_ref[TECH : TECH + 1] + step_size * (
        levbar_ref[0:1] - lev_behind + pow_behind
    )
    shift_ref[8 : 8 + rows] = sto
    shift_ref[7:8] = sto_before
    ang_step = primal_step * (flow_ref[...] + step_size * resflow_ref[...])
    ang_old = ang_ref[...] + primal_step * flow_ref[...]
    ang2_ref[...] = ang_old + ang_step
    angbar2_ref[...] = ang_old + 2.0 * ang_step
    pow_old = pownew_ref[...]
    pow_new = pow_old - primal_step * (bal + sto)
    pow2_ref[...] = pow_new
    powbar2_ref[...] = 2.0 * pow_new - pow_old
    lev_old = levnew_ref[...]
    lev_new = jnp.maximum(0.0, lev_old - primal_step * (shift_ref[7 : 7 + rows] - sto))
    lev2_ref[...] = lev_new
    levbar2_ref[...] = 2.0 * lev_new - lev_old
    squares = add_squares(
        jnp.zeros((TECH, buses), F32), ang_step, pow_new - pow_old, lev_new - lev_old
    )

    unroll = divisor(rows, 10)

    def step(t, carry, first=False, last=False):
        scaled, before, limit_sum, ramp_sum, squares = carry
        old = row_ref[...] if first else new_ref[t]
        bar_next = bar_front if last else bar_ref[t + 1]
        avail = avail_ref[t]
        scaled_next = step_size * bar_next
        lim = jnp.maximum(0.0, lim_ref[t] + (scaled - avail * cap_step))
        ramp = jnp.maximum(0.0, ramp_ref[t] + (scaled_next - scaled - ramp_cap_step))
        dual = jnp.broadcast_to(cut_ref[pl.ds(t, 1), :], (TECH, buses))
        gen = jnp.maximum(0.0, old - (cost_step + dual) - primal_step * (lim + before - ramp))
        squares += (gen - old) ** 2
        limit_sum += avail * lim
        ramp_sum += ramp
        gen2_ref[t] = gen
        lim2_ref[t] = lim
        ramp2_ref[t] = ramp
        if first:
            put_cubes(out_ref, 1, 2.0 * gen - old)
        return scaled_next, ramp, limit_sum, ramp_sum, squares

    bar = 2.0 * row_ref[...] - bar_ref[0]
    before = jnp.maximum(0.0, halo_ref[:TECH] + step_size * (bar - bar_behind - ramp_cap))
    zero = jnp.zeros((TECH, buses), F32)
    cap_step, ramp_cap_step, cost_step = step_size * cap_bar, step_size * ramp_cap, primal_step * cost
    cut_ref[...] = primal_step * bal
    carry = (step_size * bar, before, zero, zero, squares)
    for t in range(unroll):
        carry = step(t, carry, first=t == 0)

    def several(j, carry):
        for k in range(unroll):
            carry = step(j * unroll + k, carry)
        return carry

    carry = lax.fori_loop(1, rows // unroll - 1, several, carry)
    for t in range(rows - unroll, rows):
        carry = step(t, carry, last=t == rows - 1)
    _, _, limit_sum, ramp_sum, squares = carry
    put_totals(out_ref, 1, limit_sum + rate * ramp_sum, squares, (levbar2_ref[0:1],))


def residual_two_body(
    pieces, gen_ref, ang_ref, lev_ref, pow_ref, new_ref, row_ref, powbar_ref, load_ref, high_ref, low_ref, *refs,
):
    sources, refs = refs[:pieces], refs[pieces:]
    out_ref, bar_ref, gen_h, ang_h, lev_h, pow_h, sum_ref, sems = refs
    copies = [
        pltpu.make_async_copy(source, target, sems.at[k])
        for k, (source, target) in enumerate(
            ((gen_ref, gen_h), (ang_ref, ang_h), (lev_ref, lev_h), (pow_ref, pow_h))
        )
    ]
    for copy in copies:
        copy.start()
    rows, _, buses = gen_ref.shape
    unroll = divisor(rows, 7)
    flow = network_product(sources, high_ref, low_ref)

    def one(t, old):
        bar = 2.0 * gen_ref[t] - old
        bar_ref[t] = bar
        sum_ref[pl.ds(t, 1), :] = jnp.sum(bar, axis=0, keepdims=True)

    for t in range(unroll):
        one(t, new_ref[t] if t else row_ref[...])

    def several(j, _):
        for k in range(unroll):
            one(j * unroll + k, new_ref[j * unroll + k])
        return 0

    lax.fori_loop(1, rows // unroll, several, 0)
    out_ref[...] = sum_ref[...] + powbar_ref[...] - flow - load_ref[...]
    for copy in copies:
        copy.wait()


def last_body(
    hours, entries, steps, here_ref, squares_ref, other_ref, *refs,
):
    passed, refs = refs[:steps], refs[steps:]
    (
        cap_ref, inv_ref, rr_ref,
        bar_ref, lim_ref, ramp_ref, avail_ref, bal_ref, res_ref, sto_ref, levbar_ref, powbar_ref,
        cap_h, lim_h, ramp_h, bal_h, sto_h, cap_v, lim_v, ramp_v, bal_v, sto_v, shift_ref, sems, small_sems,
    ) = refs
    rows, _, buses = bar_ref.shape
    chunk = divisor(rows, 28)
    unroll = divisor(chunk, 7)
    chunks = rows // chunk
    invest, step_size = get_totals(entries, buses, 1, here_ref, squares_ref, other_ref)
    from_next = functools.partial(neighbour, passed, True)
    lev_front = get_row(buses, 1, 1, from_next)
    bar_front = get_cube(buses, 1, 0, from_next)
    cap_new = capacity_of(hours, cap_ref, inv_ref, invest)
    cap_v[...] = cap_new
    bal_v[...] = bal_ref[...] + step_size * res_ref[...]
    lev_bar = levbar_ref[...]
    shift_ref[8 : 8 + rows] = lev_bar
    shift_ref[8 + rows : 9 + rows] = lev_front
    sto_v[...] = sto_ref[...] + step_size * (shift_ref[9 : 9 + rows] - lev_bar + powbar_ref[...])
    small = [
        pltpu.make_async_copy(source, target, small_sems.at[k])
        for k, (source, target) in enumerate(((cap_v, cap_h), (bal_v, bal_h), (sto_v, sto_h)))
    ]
    for copy in small:
        copy.start()
    cap_bar = 2.0 * cap_new - cap_ref[...]
    ramp_cap = rr_ref[...] * cap_bar

    def copies(i):
        rows_here = pl.ds(i * chunk, chunk)
        return [
            pltpu.make_async_copy(source.at[rows_here], target.at[rows_here], sems.at[i, k])
            for k, (source, target) in enumerate(((lim_v, lim_h), (ramp_v, ramp_h)))
        ]

    def step(t, bar, last=False):
        bar_next = bar_front if last else bar_ref[t + 1]
        lim_v[t] = jnp.maximum(0.0, lim_ref[t] + step_size * (bar - avail_ref[t] * cap_bar))
        ramp_v[t] = jnp.maximum(0.0, ramp_ref[t] + step_size * (bar_next - bar - ramp_cap))
        return bar_next

    bar = bar_ref[0]
    for i in range(chunks):
        end = (i + 1) * chunk
        stop = end - unroll if i == chunks - 1 else end

        def several(j, bar, start=i * chunk):
            for k in range(unroll):
                bar = step(start + j * unroll + k, bar)
            return bar

        bar = lax.fori_loop(0, (stop - i * chunk) // unroll, several, bar)
        for t in range(stop, end):
            bar = step(t, bar, last=t == rows - 1)
        for copy in copies(i):
            copy.start()
    for i in range(chunks):
        for copy in copies(i):
            copy.wait()
    for copy in small:
        copy.wait()


def per_device(
    demand,
    avail_factor,
    tech_mask,
    var_cost,
    inv_cost,
    ramp_rate,
    network,
    pattern,
    live_hours,
    generation,
    angles,
    levels,
    net_power,
    capacity,
    balance_dual,
    storage_dual,
    limit_dual,
    ramp_dual,
):
    rows, buses = demand.shape
    hours = rows * lax.axis_size("hour")
    entries = float(hours * (TECH + 3) * BUS)
    swap = lax.axis_size("region") == 2
    pieces = 2 if swap else 1
    cube, flat, tech = (rows, TECH, buses), (rows, buses), (TECH, buses)
    shift = pltpu.VMEM((rows + 24, buses), F32)
    chunks = rows // divisor(rows, 28)

    def all_buses(block):
        if swap:
            return block, partner(block, "region", 1)
        return (lax.all_gather(block, "region", axis=1, tiled=True),)

    steps = len(distances("hour"))

    def totals(block, lone, once, *work):
        row = lax.broadcasted_iota(jnp.int32, block.shape, 0)
        lane = lax.broadcasted_iota(jnp.int32, block.shape, 1)
        width, parts = layout(buses, lone)
        adds = (lane < buses) | ((lane < buses + width) & (row < parts))
        passed = []
        for k, distance in enumerate(distances("hour")):
            got = partner(block, "hour", distance)
            passed.append(got)
            if k < len(work) and work[k]:
                block = after(block, work[k]())
            block = got + jnp.where(adds[:, : block.shape[1]], block, 0.0)
            if k == 0:
                block = block[:, : block.shape[1] - once]
        squares = block
        *inner, outer = distances("region")
        for distance in inner:
            squares = squares + partner(squares, "region", distance)
        return block, squares, partner(squares, "region", outer), passed

    (halo,) = call(
        pack_body,
        (ramp_dual, storage_dual, generation, limit_dual, network, avail_factor, demand, tech_mask,
         angles, net_power, levels),
        [HBM] * 11,
        [((2 * TECH, buses), F32)],
        scratch=(pltpu.VMEM((rows - (rows - 1) // TECH * TECH, buses), F32), pltpu.SemaphoreType.DMA((2,))),
        moved=1 << 28,
        name="pack",
    )
    balances = all_buses(balance_dual)
    halo = shifted(halo, "hour", 1)

    bar, new, avail, high, low, invest, square, load, flow, ang_bar, pow_new, pow_bar = call(
        functools.partial(load_body, swap),
        (generation, limit_dual, ramp_dual, avail_factor, network, tech_mask, var_cost, ramp_rate,
         balance_dual, demand, pattern, live_hours, angles, net_power, storage_dual, *balances),
        [VMEM] * 10 + [SMEM] * 2 + [VMEM] * (3 + pieces),
        [(cube, F32)] * 3 + [((buses, BUS), jnp.bfloat16)] * 2 + [(tech, F32)] * 2 + [(flat, F32)] * 5,
        name="load",
    )
    lim, ramp = limit_dual, ramp_dual
    row, lev_new, lev_bar, total = call(
        first_body,
        (bar, lim, ramp, halo, var_cost, invest, square, balance_dual, levels, storage_dual, pow_bar),
        [VMEM] * 11,
        [(tech, F32)] + [(flat, F32)] * 2 + [((TECH, 3 * buses + layout(buses, 3)[0]), F32)],
        scratch=(shift,),
        name="first",
    )
    sources = all_buses(ang_bar)
    made = {}

    def residual():
        (made["res"],) = call(
            functools.partial(residual_one_body, pieces),
            (bar, row, pow_bar, load, high, low, *sources),
            [VMEM] * (6 + pieces),
            [(flat, F32)],
            scratch=(pltpu.VMEM(flat, F32),),
            name="residual1",
        )
        return made["res"]

    def product():
        (made["flow"],) = call(
            functools.partial(product_body, pieces),
            (high, low, *all_buses(made["res"])),
            [VMEM] * (2 + pieces),
            [(flat, F32)],
            name="product",
        )
        return made["flow"]

    here, squares, other, passed = totals(total, 3, buses, None, residual, None, product)
    res, res_flow = made["res"], made["flow"]
    (
        cap, gen2, lim1, ramp1, bal1, sto1, ang2, ang_bar2, pow2, pow_bar2, lev2, lev_bar2, total2,
    ) = call(
        functools.partial(middle_body, hours, entries, steps),
        (here, squares, other, *passed, capacity, inv_cost, ramp_rate, var_cost, bar, new, row, lim, ramp, avail,
         halo, balance_dual, res, res_flow, flow, angles, pow_new, pow_bar, lev_new, lev_bar,
         storage_dual),
        [VMEM] * (24 + steps),
        [(tech, F32)] + [(cube, F32)] * 3 + [(flat, F32)] * 8 + [((TECH, 2 * buses + layout(buses, 1)[0]), F32)],
        scratch=(shift, pltpu.VMEM(flat, F32)),
        name="middle",
    )
    sources2 = all_buses(ang_bar2)

    def residual2():
        made["two"] = call(
            functools.partial(residual_two_body, pieces),
            (gen2, ang2, lev2, pow2, new, row, pow_bar2, load, high, low, *sources2),
            [VMEM] * (10 + pieces),
            [(flat, F32), (cube, F32), (cube, F32)] + [(flat, F32)] * 3,
            out_specs=[VMEM] * 2 + [HBM] * 4,
            scratch=(pltpu.VMEM(flat, F32), pltpu.SemaphoreType.DMA((4,))),
            name="residual2",
        )
        return made["two"][0]

    here2, squares2, other2, passed2 = totals(total2, 1, 0, None, residual2)
    res2, bar2, gen2, ang2, lev2, pow2 = made["two"]
    cap2, lim2, ramp2, bal2, sto2 = call(
        functools.partial(last_body, hours, entries, steps),
        (here2, squares2, other2, *passed2, cap, inv_cost, ramp_rate, bar2, lim1, ramp1, avail, bal1, res2, sto1,
         lev_bar2, pow_bar2),
        [VMEM] * (15 + steps),
        [(tech, F32), (cube, F32), (cube, F32), (flat, F32), (flat, F32)],
        out_specs=[HBM] * 5,
        scratch=(
            pltpu.VMEM(tech, F32), pltpu.VMEM(cube, F32), pltpu.VMEM(cube, F32), pltpu.VMEM(flat, F32),
            pltpu.VMEM(flat, F32), shift, pltpu.SemaphoreType.DMA((chunks, 2)), pltpu.SemaphoreType.DMA((3,)),
        ),
        name="last",
    )
    return gen2, ang2, lev2, pow2, cap2, bal2, sto2, lim2, ramp2


def solution(mesh):
    return jax.shard_map(
        per_device,
        mesh=mesh,
        in_specs=(
            P("hour", "region"),
            P("hour", None, "region"),
            P(None, "region"),
            P(None, "region"),
            P(None, "region"),
            P(None, "region"),
            P("region", None),
            P(),
            P(),
            P("hour", None, "region"),
            P("hour", "region"),
            P("hour", "region"),
            P("hour", "region"),
            P(None, "region"),
            P("hour", "region"),
            P("hour", "region"),
            P("hour", None, "region"),
            P("hour", None, "region"),
        ),
        out_specs=(
            P("hour", None, "region"),
            P("hour", "region"),
            P("hour", "region"),
            P("hour", "region"),
            P(None, "region"),
            P("hour", "region"),
            P("hour", "region"),
            P("hour", None, "region"),
            P("hour", None, "region"),
        ),
        check_vma=False,
    )
```
